128 devices in a mesh: req: 64 (over z, y, x), kv: 2 (over core).
Axes of the slice: x: 4, y: 4, z: 4, core: 2. Of those that a mesh axis runs over, the one named last changes fastest.
Arguments:
- queries: bfloat16 [16384, 2048], P(('req', 'kv')), may hold values from -6 to 6
- keys: bfloat16 [16384, 1024], P(('req', 'kv')), may hold values from -6 to 6
- values: bfloat16 [16384, 1024], P(('req', 'kv')), may hold values from -6 to 6
- residual: bfloat16 [16384, 3584], P(('req', 'kv'))
- segment_ids: int32 [16384], P(('req', 'kv')), may hold values from 127 to 16383, as said below
- regroup: int32 [16384], P(('req', 'kv')), may hold values from 0 to 16383, as said below
- out_weight: bfloat16 [2048, 3584], P('kv')
- attn_gain: float32 [3584], replicated, may hold values from 0.1 to 1.9
- pre_gain: float32 [3584], replicated, may hold values from 0.1 to 1.9
- gate_weight: bfloat16 [3584, 7168], P(None, 'kv'), may hold values from -0.09375 to 0.09375
- up_weight: bfloat16 [3584, 7168], P(None, 'kv'), may hold values from -0.09375 to 0.09375
- down_weight: bfloat16 [7168, 3584], P('kv')
- post_gain: float32 [3584], replicated, may hold values from 0.1 to 1.9
Outputs:
- layer_out: bfloat16 [16384, 3584], P(('req', 'kv'))
- key_cache_rows: bfloat16 [4, 16384, 256], P(None, ('req', 'kv'))
- value_cache_rows: bfloat16 [4, 16384, 256], P(None, ('req', 'kv'))
The draws below stay inside these ranges and needn't reach their ends.
Inputs may be any that keep to these rules, and one draw needn't show every extreme that they name: `segment_ids`: A request is a run of consecutive slots carrying one id, the index of its last slot; no request runs from one index of req's 256 slots into the next. `regroup`: A permutation of the slots. Each device (in req+kv order) sends exactly one of its 128 slots to each of the 128 devices: for every pair of devices, exactly one slot of the first has its output row among the 128 rows of the second.
All inputs are finite; a program needn't handle non-finite values.
Results may differ from the reference program's by a relative error of at most 0.0095.
Values may be sent and summed in bfloat16 or wider, within the bound.
A program may use at most 192 MiB of HBM per device.

```python
import math
import jax
import jax.numpy as jnp
from jax import lax

MODEL_WIDTH = 3584
FF = 7168
QUERY_HEADS = 8
KEY_VALUE_HEADS = 4
HEAD_ENTRIES = 256
WINDOW_REACH = 512
TOKEN_SLOTS_PART = 128
GROUP = 256
TOTAL_SLOTS = 16384
N_KV = 2


def scaled_scores(key, row_count, col_count, row_log):
    part_keys = jax.random.split(key, 3)
    col_scale = jnp.exp(jax.random.uniform(part_keys[0], (1, col_count), jnp.float32, 0.0, math.log(10.0)))
    row_scale = jnp.exp(jax.random.uniform(part_keys[1], (row_count, 1), jnp.float32, 0.0, row_log))
    base_draw = jax.random.normal(part_keys[2], (row_count, col_count), jnp.float32)
    return base_draw * col_scale * row_scale


def draw_residual(key, part):
    score_matrix = scaled_scores(jax.random.fold_in(key, 1), TOTAL_SLOTS, MODEL_WIDTH, math.log(10.0))
    return (score_matrix / 8.0).astype(jnp.bfloat16)


def draw_out_weight(key, part):
    score_matrix = scaled_scores(jax.random.fold_in(key, 2), QUERY_HEADS * HEAD_ENTRIES, MODEL_WIDTH, 0.0)
    return (score_matrix * (QUERY_HEADS * HEAD_ENTRIES) ** (-0.5) / 4.0).astype(jnp.bfloat16)


def draw_down_weight(key, part):
    score_matrix = scaled_scores(jax.random.fold_in(key, 3), FF, MODEL_WIDTH, 0.0)
    return (score_matrix * FF ** (-0.5) / 4.0).astype(jnp.bfloat16)


def draw_segment_ids(key, part):
    random_sample = jax.random.randint(jax.random.fold_in(key, 5), (TOTAL_SLOTS,), 0, 32)
    token_slot_index = jnp.arange(TOTAL_SLOTS, dtype=jnp.int32)
    local_index = token_slot_index % GROUP
    first_end = GROUP // 2 - 1
    sequence_end_flags = (local_index == GROUP - 1) | (random_sample == 0) & (token_slot_index > first_end) | (token_slot_index == first_end)
    sequence_end_marks = jnp.where(sequence_end_flags, token_slot_index, TOTAL_SLOTS)
    return lax.cummin(sequence_end_marks, axis=0, reverse=True).astype(jnp.int32)


def one_permutation(sub_key):
    return jax.random.permutation(sub_key, TOKEN_SLOTS_PART)


def draw_regroup(key, part):
    device_list = TOTAL_SLOTS // TOKEN_SLOTS_PART
    per_peer = TOKEN_SLOTS_PART // device_list
    first_key, second_key = jax.random.split(jax.random.fold_in(key, 7))
    sender = jax.vmap(one_permutation)(jax.random.split(first_key, device_list)).astype(jnp.int32)
    receiver = jax.vmap(one_permutation)(jax.random.split(second_key, device_list)).astype(jnp.int32)
    target_device = sender // per_peer
    arrival = jnp.arange(device_list, dtype=jnp.int32)[:, None] * per_peer + sender % per_peer
    slot_ids = receiver[target_device, arrival]
    return (target_device * TOKEN_SLOTS_PART + slot_ids).reshape(-1).astype(jnp.int32)


def block_levels(own_key, dims, pieces, low, high):
    def one(axis_at, parts):
        draws = jax.random.uniform(jax.random.fold_in(jax.random.fold_in(own_key, 6), axis_at), (parts,), jnp.float32, low / len(pieces), high / len(pieces))
        return jnp.repeat(jnp.exp(draws), dims[axis_at] // parts).reshape((-1,) + (1,) * (len(dims) - axis_at - 1))

    gain = one(*pieces[0])
    for cut in pieces[1:]:
        gain = gain * one(*cut)
    return gain


def scatter_about(own_key, dims, width, bound, cuts=(), held_as=jnp.bfloat16):
    result = width * jax.random.normal(own_key, dims, jnp.float32)
    if cuts:
        result = result * block_levels(own_key, dims, cuts, -0.22, 0.18)
    return jnp.clip(result, -bound, bound).astype(held_as)


def setup_inputs(seed: int = 0) -> dict:
    key_list = jax.random.split(jax.random.key(seed), 14)
    queries = scatter_about(key_list[0], (TOTAL_SLOTS, QUERY_HEADS * HEAD_ENTRIES), 1.0, 6.0, ((0, 128),))
    keys = scatter_about(key_list[1], (TOTAL_SLOTS, KEY_VALUE_HEADS * HEAD_ENTRIES), 1.0, 6.0, ((0, 128),))
    values = scatter_about(key_list[2], (TOTAL_SLOTS, KEY_VALUE_HEADS * HEAD_ENTRIES), 1.0, 6.0, ((0, 128),))
    residual = draw_residual(jax.random.fold_in(key_list[13], 71), 0)
    segment_ids = draw_segment_ids(jax.random.fold_in(key_list[13], 71), 0)
    regroup = draw_regroup(jax.random.fold_in(key_list[13], 71), 0)
    out_weight = draw_out_weight(jax.random.fold_in(key_list[13], 71), 0)
    attn_gain = jnp.clip(1.0 + 0.18 * jax.random.normal(key_list[7], (MODEL_WIDTH,), jnp.float32), 0.1, 1.9)
    pre_gain = jnp.clip(1.0 + 0.18 * jax.random.normal(key_list[8], (MODEL_WIDTH,), jnp.float32), 0.1, 1.9)
    gate_weight = scatter_about(key_list[9], (MODEL_WIDTH, FF), MODEL_WIDTH ** -0.5, 0.09375, ((1, 2),))
    up_weight = scatter_about(key_list[10], (MODEL_WIDTH, FF), MODEL_WIDTH ** -0.5, 0.09375, ((1, 2),))
    down_weight = draw_down_weight(jax.random.fold_in(key_list[13], 71), 0)
    post_gain = jnp.clip(1.0 + 0.18 * jax.random.normal(key_list[12], (MODEL_WIDTH,), jnp.float32), 0.1, 1.9)
    return {"queries": queries, "keys": keys, "values": values, "residual": residual, "segment_ids": segment_ids, "regroup": regroup, "out_weight": out_weight, "attn_gain": attn_gain, "pre_gain": pre_gain, "gate_weight": gate_weight, "up_weight": up_weight, "down_weight": down_weight, "post_gain": post_gain}


cap_value = 50.0
norm_eps = 1e-06

def rms_scale(values_in, gain_row):
    mean_square = lax.optimization_barrier(jnp.mean(values_in * values_in, axis=-1, keepdims=True))
    return values_in * lax.rsqrt(mean_square + norm_eps) * gain_row

def round_trip(values_in):
    return lax.optimization_barrier(values_in.astype(jnp.bfloat16)).astype(jnp.float32)

def reference(queries, keys, values, residual, segment_ids, regroup, out_weight, attn_gain, pre_gain, gate_weight, up_weight, down_weight, post_gain):
    grouped_heads = QUERY_HEADS // KEY_VALUE_HEADS
    query_tile_block = 512
    keys_padded_full = jnp.concatenate([jnp.zeros((WINDOW_REACH, KEY_VALUE_HEADS * HEAD_ENTRIES), keys.dtype), keys], axis=0)
    values_padded_full = jnp.concatenate([jnp.zeros((WINDOW_REACH, KEY_VALUE_HEADS * HEAD_ENTRIES), values.dtype), values], axis=0)
    padded_ids = jnp.concatenate([jnp.full((WINDOW_REACH,), -1, jnp.int32), segment_ids.astype(jnp.int32)], axis=0)

    def attend_window(block_index):
        leading_row = (block_index * query_tile_block).astype(jnp.int32)
        query_portion = lax.dynamic_slice_in_dim(queries, leading_row, query_tile_block, 0).astype(jnp.float32).reshape(query_tile_block, KEY_VALUE_HEADS, grouped_heads, HEAD_ENTRIES)
        key_portion = lax.dynamic_slice_in_dim(keys_padded_full, leading_row, WINDOW_REACH + query_tile_block, 0).astype(jnp.float32).reshape(WINDOW_REACH + query_tile_block, KEY_VALUE_HEADS, HEAD_ENTRIES)
        value_portion = lax.dynamic_slice_in_dim(values_padded_full, leading_row, WINDOW_REACH + query_tile_block, 0).astype(jnp.float32).reshape(WINDOW_REACH + query_tile_block, KEY_VALUE_HEADS, HEAD_ENTRIES)
        query_ids = lax.dynamic_slice_in_dim(segment_ids.astype(jnp.int32), leading_row, query_tile_block, 0)
        key_ids = lax.dynamic_slice_in_dim(padded_ids, leading_row, WINDOW_REACH + query_tile_block, 0)
        raw_scores = jnp.einsum('tkgd,skd->kgts', query_portion, key_portion, precision=lax.Precision.HIGHEST)
        scores = cap_value * jnp.tanh(raw_scores * HEAD_ENTRIES ** (-0.5) / cap_value)
        distance = jnp.arange(query_tile_block, dtype=jnp.int32)[:, None] + WINDOW_REACH - jnp.arange(WINDOW_REACH + query_tile_block, dtype=jnp.int32)[None, :]
        allowed = (query_ids[:, None] == key_ids[None, :]) & (distance >= 0) & (distance < WINDOW_REACH)
        weights = jnp.where(allowed, jnp.exp(scores), 0.0)
        totals = lax.optimization_barrier(jnp.sum(weights, axis=-1))
        rounded = round_trip(weights)
        numerator = jnp.einsum('kgts,skd->tkgd', rounded, value_portion, precision=lax.Precision.HIGHEST)
        mixed_heads = numerator / jnp.transpose(totals, (2, 0, 1))[..., None]
        return mixed_heads.astype(jnp.bfloat16).reshape(query_tile_block, QUERY_HEADS * HEAD_ENTRIES)
    attended_output = lax.map(attend_window, jnp.arange(TOTAL_SLOTS // query_tile_block, dtype=jnp.int32)).reshape(TOTAL_SLOTS, QUERY_HEADS * HEAD_ENTRIES)
    kv_part = QUERY_HEADS * HEAD_ENTRIES // N_KV
    hidden_part = FF // N_KV
    out_split = out_weight.astype(jnp.float32).reshape(N_KV, kv_part, MODEL_WIDTH)
    down_split = down_weight.astype(jnp.float32).reshape(N_KV, hidden_part, MODEL_WIDTH)
    row_tile_block = 1024

    def relayed_rows(operands):
        attended_rows, residual_rows = operands
        attn_parts = jnp.einsum('rkc,kcd->krd', attended_rows.astype(jnp.float32).reshape(row_tile_block, N_KV, kv_part), out_split, precision=lax.Precision.HIGHEST)
        projected = lax.optimization_barrier(jnp.sum(round_trip(attn_parts), axis=0))
        stream = (residual_rows.astype(jnp.float32) + rms_scale(projected, attn_gain)).astype(jnp.bfloat16)
        normed = rms_scale(stream.astype(jnp.float32), pre_gain).astype(jnp.bfloat16)
        gate_part = jnp.dot(normed, gate_weight, preferred_element_type=jnp.float32)
        up_part = jnp.dot(normed, up_weight, preferred_element_type=jnp.float32)
        active = (jax.nn.gelu(gate_part, approximate=True) * up_part).astype(jnp.bfloat16)
        ffw_parts = jnp.einsum('rkc,kcd->krd', active.astype(jnp.float32).reshape(row_tile_block, N_KV, hidden_part), down_split, precision=lax.Precision.HIGHEST)
        ffw_sum = lax.optimization_barrier(jnp.sum(round_trip(ffw_parts), axis=0))
        return (stream.astype(jnp.float32) + rms_scale(ffw_sum, post_gain)).astype(jnp.bfloat16)
    output_rows = lax.map(relayed_rows, (attended_output.reshape(TOTAL_SLOTS // row_tile_block, row_tile_block, QUERY_HEADS * HEAD_ENTRIES), residual.reshape(TOTAL_SLOTS // row_tile_block, row_tile_block, MODEL_WIDTH))).reshape(TOTAL_SLOTS, MODEL_WIDTH)
    destination_rows = regroup.astype(jnp.int32)
    layer_out = jnp.zeros_like(output_rows).at[destination_rows].set(output_rows)
    key_cache_rows = jnp.zeros_like(keys).at[destination_rows].set(keys).reshape(TOTAL_SLOTS, KEY_VALUE_HEADS, HEAD_ENTRIES).transpose(1, 0, 2)
    value_cache_rows = jnp.zeros_like(values).at[destination_rows].set(values).reshape(TOTAL_SLOTS, KEY_VALUE_HEADS, HEAD_ENTRIES).transpose(1, 0, 2)
    return (layer_out, key_cache_rows, value_cache_rows)
```

```python
import jax
import jax.numpy as jnp
from jax import lax
from jax.experimental import pallas as pl
from jax.experimental.pallas import tpu as pltpu
from jax.sharding import PartitionSpec as P

MESH = pl.DeviceIdType.MESH
CHIPS = 64
SIDE = 4
ROWS = 128
WIDTH = 3584
HEAD = 256
OWN_HEADS = 4
HALF = 1024
KV_HALF = 512
KV_WIDTH = 2048
CHUNK = 512
CHUNKS = WIDTH // CHUNK
SLOTS = 10
GROUPS = 8
PER_GROUP = CHIPS // GROUPS
CAP = 50.0
EPS = 1e-06
BF = jnp.bfloat16
F32 = jnp.float32


def cols(j, width=CHUNK):
    return pl.ds(pl.multiple_of(j * width, width), width)


def rows_of(core):
    return pl.ds(pl.multiple_of(core * ROWS, ROWS), ROWS)


def kernel(
    q, k, v, res, seg, rg, ow, ag, pg, gw, uw, dw, og,
    lo, kc, vc,
    wbuf, qb, kb, vb, segb, kvl, rgb, gains, rb, att, part, prec, pkv, kvr, pks, strr,
    pb, xb, act, drec, kvo, pf,
    in_sem, o_sem, w_sem, out_sem, ex_send, ex_recv, pr_send, pr_recv, dn_send, dn_recv,
    kv_send, kv_recv, kvf_send, kvf_recv, st_send, st_recv, stf_send, stf_recv,
):
    chip = lax.axis_index("req")
    core = lax.axis_index("kv")
    other = 1 - core
    sibling = (chip, other)
    z, y, x = lax.div(chip, 16), lax.rem(lax.div(chip, 4), 4), lax.rem(chip, 4)

    def chip_at(i):
        zz = lax.rem(z + lax.div(i, 16), 4)
        yy = lax.rem(y + lax.rem(lax.div(i, 4), 4), 4)
        xx = lax.rem(x + lax.rem(i, 4), 4)
        return zz * 16 + yy * 4 + xx

    def local(src, dst, sem):
        return pltpu.make_async_copy(src, dst, sem)

    def remote(src, dst, send, recv, device):
        return pltpu.make_async_remote_copy(
            src_ref=src, dst_ref=dst, send_sem=send, recv_sem=recv, device_id=device, device_id_type=MESH
        )

    barrier = pltpu.get_barrier_semaphore()
    pl.semaphore_signal(barrier, inc=1, device_id=sibling, device_id_type=MESH)

    def greet(i, c):
        pl.semaphore_signal(barrier, inc=1, device_id=(chip_at(i), core), device_id_type=MESH)
        return c

    lax.fori_loop(1, CHIPS, greet, 0)

    ins = [
        local(rg, rgb, in_sem.at[0]),
        local(k, kvl.at[:, pl.ds(0, HALF)], in_sem.at[1]),
        local(v, kvl.at[:, pl.ds(HALF, HALF)], in_sem.at[2]),
        local(seg, segb.at[core], in_sem.at[3]),
        local(q.at[:, cols(core, HALF)], qb.at[rows_of(core), :], in_sem.at[4]),
        local(k.at[:, cols(core, KV_HALF)], kb.at[rows_of(core), :], in_sem.at[5]),
        local(v.at[:, cols(core, KV_HALF)], vb.at[rows_of(core), :], in_sem.at[6]),
        local(ag, gains.at[0], in_sem.at[7]),
        local(pg, gains.at[1], in_sem.at[8]),
        local(og, gains.at[2], in_sem.at[9]),
        local(res, rb, in_sem.at[10]),
    ]
    for c in ins:
        c.start()

    def o_load(j):
        return local(ow.at[:, cols(j)], wbuf.at[pl.ds(pl.multiple_of(j * HALF, HALF), HALF), :], o_sem.at[j])

    for j in range(CHUNKS):
        o_load(j).start()

    def w_load(src, j, unit):
        slot = lax.rem(unit, SLOTS) if not isinstance(unit, int) else unit % SLOTS
        return local(
            src.at[:, cols(j)],
            wbuf.at[pl.ds(pl.multiple_of(slot * WIDTH, WIDTH), WIDTH), :],
            w_sem.at[slot],
        )

    for c in ins[:3]:
        c.wait()
    to = rgb[...]
    pick = lax.broadcasted_iota(jnp.int32, (ROWS, ROWS), 0) == lax.shift_right_logical(to, 7)
    pos = jnp.sum(
        jnp.where(pick, jnp.bitwise_and(to, 255).astype(F32), 0.0), axis=1, keepdims=True
    )
    pick = pick.astype(BF)
    pkv[:, :, KV_WIDTH:] = jnp.broadcast_to(pos, (ROWS, ROWS)).astype(BF).reshape(CHIPS, 2, ROWS)
    for j in range(KV_WIDTH // CHUNK):
        y_rows = jnp.dot(pick, kvl[:, cols(j)], preferred_element_type=F32).astype(BF)
        pkv[:, :, cols(j)] = y_rows.reshape(CHIPS, 2, CHUNK)

    pl.semaphore_wait(barrier, CHIPS)

    exchange = [
        remote(seg, segb.at[core], ex_send.at[0], ex_recv.at[0], sibling),
        remote(
            q.at[:, cols(other, HALF)], qb.at[rows_of(core), :], ex_send.at[1], ex_recv.at[1], sibling
        ),
        remote(
            k.at[:, cols(other, KV_HALF)], kb.at[rows_of(core), :], ex_send.at[2], ex_recv.at[2], sibling
        ),
        remote(
            v.at[:, cols(other, KV_HALF)], vb.at[rows_of(core), :], ex_send.at[3], ex_recv.at[3], sibling
        ),
    ]
    for c in exchange:
        c.start()

    def scatter(packets, landing, send, recv):
        here = local(packets.at[chip], landing.at[core, 0], recv.at[0])
        here.start()

        def one(i, c):
            there = chip_at(i)
            remote(
                packets.at[there], landing.at[core, i], send, recv.at[lax.div(i, PER_GROUP)], (there, core)
            ).start()
            return c

        lax.fori_loop(1, CHIPS, one, 0)

    def scattered(packets, landing, send, recv):
        remote(
            packets.at[pl.ds(0, CHIPS - 1)], landing.at[core, pl.ds(0, CHIPS - 1)], send, recv.at[0], sibling
        ).wait_send()

    def group(i):
        return pl.ds(i * PER_GROUP, PER_GROUP)

    def forward(landing, i, send, recv):
        return remote(
            landing.at[core, group(i)], landing.at[core, group(i)], send.at[i], recv.at[i], sibling
        )

    def hand_on(landing, recv, send_f, recv_f):
        def one(i, c):
            block = landing.at[core, group(i)]
            local(block, block, recv.at[i]).wait()
            forward(landing, i, send_f, recv_f).start()
            return c

        lax.fori_loop(0, GROUPS, one, 0)

        def arrived(i, c):
            theirs = landing.at[other, group(i)]
            remote(theirs, theirs, send_f.at[i], recv_f.at[i], sibling).wait_recv()
            return c

        lax.fori_loop(0, GROUPS, arrived, 0)

    scatter(pkv, kvr, kv_send, kv_recv)

    for unit in range(2, SLOTS):
        w_load(gw if unit % 2 == 0 else uw, (unit - 2) // 2, unit).start()

    for c in ins[3:]:
        c.wait()
    for c in exchange:
        c.wait_recv()
    two = 2 * ROWS
    t_at = lax.broadcasted_iota(jnp.int32, (two, two), 0)
    s_at = lax.broadcasted_iota(jnp.int32, (two, two), 1)
    last = jnp.concatenate([segb[0], segb[1]], axis=1) - chip * two
    allowed = (s_at <= t_at) & (last >= t_at)
    for h in range(OWN_HEADS):
        own = pl.ds(h * HEAD, HEAD)
        key = pl.ds(h // 2 * HEAD, HEAD)
        raw = lax.dot_general(
            qb[:, own], kb[:, key], (((1,), (1,)), ((), ())), preferred_element_type=F32
        )
        scores = CAP * jnp.tanh(raw * (HEAD**-0.5 / CAP))
        probs = jnp.where(allowed, jnp.exp(scores), 0.0)
        totals = jnp.sum(probs, axis=-1, keepdims=True)
        mixed = jnp.dot(probs.astype(BF), vb[:, key], preferred_element_type=F32)
        att[:, own] = (mixed * (1.0 / totals)).astype(BF)

    def halves(landing, j, send, recv):
        return remote(
            part.at[rows_of(other), cols(j)], landing.at[:, cols(j)], send.at[j], recv.at[j], sibling
        )

    def project(j, c):
        o_load(j).wait()
        w = wbuf[pl.ds(pl.multiple_of(j * HALF, HALF), HALF), :]
        part[:, cols(j)] = jnp.dot(att[...], w, preferred_element_type=F32).astype(BF)
        halves(prec, j, pr_send, pr_recv).start()
        return c

    lax.fori_loop(0, CHUNKS, project, 0)
    w_load(gw, 4, SLOTS).start()
    w_load(uw, 4, SLOTS + 1).start()

    def lanes_sum(value):
        total = value[:, 0:128]
        for i in range(1, CHUNK // 128):
            total = total + value[:, i * 128 : (i + 1) * 128]
        return total

    def sum_halves(landing, send, recv):
        def one(j, squares):
            halves(landing, j, send, recv).wait_recv()
            both = part[rows_of(core), cols(j)].astype(F32) + landing[:, cols(j)].astype(F32)
            pf[:, cols(j)] = both
            return squares + lanes_sum(both * both)

        squares = lax.fori_loop(0, CHUNKS, one, jnp.zeros((ROWS, 128), F32))
        return lax.rsqrt(jnp.sum(squares, axis=-1, keepdims=True) * (1.0 / WIDTH) + EPS)

    scale = sum_halves(prec, pr_send, pr_recv)

    def to_packets(j, c):
        stream = (rb[:, cols(j)].astype(F32) + pf[:, cols(j)] * scale * gains[0, :, cols(j)]).astype(BF)
        y_rows = jnp.dot(pick, stream, preferred_element_type=F32).astype(BF)
        pks[:, :, cols(j)] = y_rows.reshape(CHIPS, 2, CHUNK)
        return c

    lax.fori_loop(0, CHUNKS, to_packets, 0)
    scatter(pks, strr, st_send, st_recv)

    hand_on(kvr, kv_recv, kvf_send, kvf_recv)
    at = kvr[:, :, :, KV_WIDTH:].reshape(two, 128).astype(F32)
    at = jnp.transpose(at)[0:1, :].astype(jnp.int32)
    place = (t_at == at).astype(BF)
    own_place = (t_at[0:ROWS, :] + core * ROWS == at).astype(BF)
    for j in range(KV_WIDTH // CHUNK):
        got = jnp.dot(
            own_place, kvr[:, :, :, cols(j)].reshape(two, CHUNK), preferred_element_type=F32
        ).astype(BF)
        kvo[2 * j] = got[:, 0:HEAD]
        kvo[2 * j + 1] = got[:, HEAD:]
    outs = [
        local(kvo.at[pl.ds(0, 4)], kc, out_sem.at[0]),
        local(kvo.at[pl.ds(4, 4)], vc, out_sem.at[1]),
    ]
    for c in outs:
        c.start()

    hand_on(strr, st_recv, stf_send, stf_recv)

    def put(j, squares):
        got = jnp.dot(
            place, strr[:, :, :, cols(j)].reshape(two, CHUNK), preferred_element_type=F32
        )
        pb[:, cols(j)] = got.astype(BF)
        return squares + lanes_sum(got * got)

    squares = lax.fori_loop(0, CHUNKS, put, jnp.zeros((two, 128), F32))
    scale = lax.rsqrt(jnp.sum(squares, axis=-1, keepdims=True) * (1.0 / WIDTH) + EPS)

    def norm(j, c):
        xb[:, cols(j)] = (pb[:, cols(j)].astype(F32) * scale * gains[1, :, cols(j)]).astype(BF)
        return c

    lax.fori_loop(0, CHUNKS, norm, 0)

    def weight(unit, i):
        slot = lax.rem(unit, SLOTS)
        return wbuf[
            pl.ds(pl.multiple_of(slot * WIDTH, WIDTH), WIDTH), pl.ds(i * 256, 256)
        ]

    def loaded(unit):
        slot = lax.rem(unit, SLOTS)
        block = wbuf.at[pl.ds(pl.multiple_of(slot * WIDTH, WIDTH), WIDTH), :]
        local(block, block, w_sem.at[slot]).wait()

    def hidden(j, c):
        loaded(2 + 2 * j)
        loaded(3 + 2 * j)
        for i in range(CHUNK // 256):
            u = jnp.dot(xb[...], weight(2 + 2 * j, i), preferred_element_type=F32)
            up = jnp.dot(xb[...], weight(3 + 2 * j, i), preferred_element_type=F32)
            gelu = 0.5 * u * (1.0 + jnp.tanh(0.7978845608028654 * (u + 0.044715 * (u * u * u))))
            act[:, pl.ds(pl.multiple_of(j * CHUNK + i * 256, 256), 256)] = (gelu * up).astype(BF)

        @pl.when(j < 2)
        def _():
            w_load(gw, 5 + j, 12 + 2 * j).start()
            w_load(uw, 5 + j, 13 + 2 * j).start()

        @pl.when((j >= 2) & (j < 6))
        def _():
            w_load(dw, 2 * (j - 2), 12 + 2 * j).start()

        @pl.when((j >= 2) & (j < 5))
        def _():
            w_load(dw, 2 * (j - 2) + 1, 13 + 2 * j).start()

        return c

    lax.fori_loop(0, CHUNKS, hidden, 0)

    def projected(j, c):
        halves(prec, j, pr_send, pr_recv).wait_send()
        return c

    lax.fori_loop(0, CHUNKS, projected, 0)

    def down(j, c):
        loaded(16 + j)
        for i in range(CHUNK // 256):
            got = jnp.dot(act[...], weight(16 + j, i), preferred_element_type=F32)
            part[:, pl.ds(pl.multiple_of(j * CHUNK + i * 256, 256), 256)] = got.astype(BF)
        halves(drec, j, dn_send, dn_recv).start()
        return c

    lax.fori_loop(0, CHUNKS, down, 0)
    scale = sum_halves(drec, dn_send, dn_recv)

    def finish(j, c):
        rb[:, cols(j)] = (
            pb[rows_of(core), cols(j)].astype(F32) + pf[:, cols(j)] * scale * gains[2, :, cols(j)]
        ).astype(BF)
        return c

    lax.fori_loop(0, CHUNKS, finish, 0)
    last_out = local(rb, lo, out_sem.at[2])
    last_out.start()

    for c in exchange:
        c.wait_send()
    scattered(pkv, kvr, kv_send, kv_recv)
    scattered(pks, strr, st_send, st_recv)

    def sent(i, c):
        forward(kvr, i, kvf_send, kvf_recv).wait_send()
        forward(strr, i, stf_send, stf_recv).wait_send()
        return c

    lax.fori_loop(0, GROUPS, sent, 0)

    def down_sent(j, c):
        halves(drec, j, dn_send, dn_recv).wait_send()
        return c

    lax.fori_loop(0, CHUNKS, down_sent, 0)
    for c in outs:
        c.wait()
    last_out.wait()


def per_device(
    queries,
    keys,
    values,
    residual,
    segment_ids,
    regroup,
    out_weight,
    attn_gain,
    pre_gain,
    gate_weight,
    up_weight,
    down_weight,
    post_gain,
):
    dma = pltpu.SemaphoreType.DMA
    vmem = pltpu.VMEM
    return pl.pallas_call(
        kernel,
        out_shape=(
            jax.ShapeDtypeStruct((ROWS, WIDTH), BF),
            jax.ShapeDtypeStruct((4, ROWS, HEAD), BF),
            jax.ShapeDtypeStruct((4, ROWS, HEAD), BF),
        ),
        in_specs=[pl.BlockSpec(memory_space=pl.ANY)] * 13,
        out_specs=(pl.BlockSpec(memory_space=pl.ANY),) * 3,
        scratch_shapes=[
            vmem((SLOTS * WIDTH, CHUNK), BF),
            vmem((2 * ROWS, HALF), BF),
            vmem((2 * ROWS, KV_HALF), BF),
            vmem((2 * ROWS, KV_HALF), BF),
            vmem((2, 1, ROWS), jnp.int32),
            vmem((ROWS, KV_WIDTH), BF),
            vmem((1, ROWS), jnp.int32),
            vmem((3, 1, WIDTH), F32),
            vmem((ROWS, WIDTH), BF),
            vmem((2 * ROWS, HALF), BF),
            vmem((2 * ROWS, WIDTH), BF),
            vmem((ROWS, WIDTH), BF),
            vmem((CHIPS, 2, KV_WIDTH + 128), BF),
            vmem((2, CHIPS, 2, KV_WIDTH + 128), BF),
            vmem((CHIPS, 2, WIDTH), BF),
            vmem((2, CHIPS, 2, WIDTH), BF),
            vmem((2 * ROWS, WIDTH), BF),
            vmem((2 * ROWS, WIDTH), BF),
            vmem((2 * ROWS, WIDTH), BF),
            vmem((ROWS, WIDTH), BF),
            vmem((8, ROWS, HEAD), BF),
            vmem((ROWS, WIDTH), F32),
            dma((11,)),
            dma((CHUNKS,)),
            dma((SLOTS,)),
            dma((3,)),
            dma((4,)),
            dma((4,)),
            dma((CHUNKS,)),
            dma((CHUNKS,)),
            dma((CHUNKS,)),
            dma((CHUNKS,)),
            dma,
            dma((GROUPS,)),
            dma((GROUPS,)),
            dma((GROUPS,)),
            dma,
            dma((GROUPS,)),
            dma((GROUPS,)),
            dma((GROUPS,)),
        ],
        compiler_params=pltpu.CompilerParams(
            collective_id=0, has_side_effects=True, vmem_limit_bytes=62 * 1024 * 1024
        ),
        name="layer",
    )(
        queries,
        keys,
        values,
        residual,
        segment_ids.reshape(1, ROWS),
        regroup.reshape(1, ROWS),
        out_weight,
        attn_gain.reshape(1, WIDTH),
        pre_gain.reshape(1, WIDTH),
        gate_weight,
        up_weight,
        down_weight,
        post_gain.reshape(1, WIDTH),
    )


def solution(mesh):
    rows = P(("req", "kv"), None)
    flat = P(("req", "kv"))
    return jax.shard_map(
        per_device,
        mesh=mesh,
        in_specs=(
            rows, rows, rows, rows, flat, flat, P("kv", None), P(), P(),
            P(None, "kv"), P(None, "kv"), P("kv", None), P(),
        ),
        out_specs=(rows, P(None, ("req", "kv"), None), P(None, ("req", "kv"), None)),
        check_vma=False,
    )
```

```python
import jax
import jax.numpy as jnp
from jax import lax
from jax.experimental import pallas as pl
from jax.experimental.pallas import tpu as pltpu
from jax.sharding import PartitionSpec as P

MESH = pl.DeviceIdType.MESH
CHIPS = 64
SIDE = 4
ROWS = 128
WIDTH = 3584
HEAD = 256
OWN_HEADS = 4
HALF = 1024
KV_HALF = 512
KV_WIDTH = 2048
CHUNK = 512
CHUNKS = WIDTH // CHUNK
SLOTS = 10
GROUPS = 8
PER_GROUP = CHIPS // GROUPS
CAP = 50.0
EPS = 1e-06
BF = jnp.bfloat16
F32 = jnp.float32


def cols(j, width=CHUNK):
    if isinstance(j, int):
        return pl.ds(j * width, width)
    return pl.ds(pl.multiple_of(j * width, width), width)


def rows_of(core):
    return pl.ds(pl.multiple_of(core * ROWS, ROWS), ROWS)


def lanes_sum(value):
    total = value[:, 0:128]
    for i in range(1, CHUNK // 128):
        total = total + value[:, i * 128 : (i + 1) * 128]
    return total


def kernel(
    q, k, v, res, seg, rg, ow, ag, pg, gw, uw, dw,
    mine, theirs, own_rows, kvo,
    wbuf, qb, kb, vb, segb, kvl, rgb, ag_row, pg_row, rb, att, part, prec, pkv, kvr, pks, strr,
    pb, xb, act, kvb, pf,
    in_sem, o_sem, w_sem, out_sem, keep_sem, ex_send, ex_recv, pr_send, pr_recv, dn_send, dn_recv,
    kv_send, kv_recv, kvf_send, kvf_recv, st_send, st_recv, stf_send, stf_recv,
):
    chip = lax.axis_index("req")
    core = lax.axis_index("kv")
    other = 1 - core
    sibling = (chip, other)
    z = lax.div(chip, SIDE * SIDE)
    plane = chip - z * (SIDE * SIDE)
    y = lax.div(plane, SIDE)
    x = plane - y * SIDE

    def wrap(at):
        return jnp.where(at >= SIDE, at - SIDE, at)

    across = [wrap(x + n) for n in range(SIDE)]

    def each_chip(do):
        def outer(a, za):
            def inner(b, yb):
                for n in range(SIDE):
                    there = wrap(za + n) * (SIDE * SIDE) + wrap(yb + n) * SIDE + across[n]
                    if n == 0:

                        @pl.when(a + b > 0)
                        def _():
                            do(a * (SIDE * SIDE) + b * SIDE, there)
                    else:
                        do(a * (SIDE * SIDE) + b * SIDE + n, there)
                return wrap(yb + 1)

            lax.fori_loop(0, SIDE, inner, y)
            return wrap(za + 1)

        lax.fori_loop(0, SIDE, outer, z)

    def local(src, dst, sem):
        return pltpu.make_async_copy(src, dst, sem)

    def remote(src, dst, send, recv, device):
        return pltpu.make_async_remote_copy(
            src_ref=src, dst_ref=dst, send_sem=send, recv_sem=recv, device_id=device, device_id_type=MESH
        )

    barrier = pltpu.get_barrier_semaphore()
    pl.semaphore_signal(barrier, inc=1, device_id=sibling, device_id_type=MESH)

    def greet(i, there):
        pl.semaphore_signal(barrier, inc=1, device_id=(there, core), device_id_type=MESH)

    each_chip(greet)

    ins = [
        local(rg, rgb, in_sem.at[0]),
        local(k, kvl.at[:, pl.ds(0, HALF)], in_sem.at[1]),
        local(v, kvl.at[:, pl.ds(HALF, HALF)], in_sem.at[2]),
        local(seg, segb.at[core], in_sem.at[3]),
        local(q.at[:, cols(core, HALF)], qb.at[rows_of(core), :], in_sem.at[4]),
        local(k.at[:, cols(core, KV_HALF)], kb.at[rows_of(core), :], in_sem.at[5]),
        local(v.at[:, cols(core, KV_HALF)], vb.at[rows_of(core), :], in_sem.at[6]),
        local(ag, ag_row, in_sem.at[7]),
        local(pg, pg_row, in_sem.at[8]),
        local(res, rb, in_sem.at[9]),
    ]
    for c in ins:
        c.start()

    def o_load(j):
        return local(ow.at[:, cols(j)], wbuf.at[pl.ds(pl.multiple_of(j * HALF, HALF), HALF), :], o_sem.at[j])

    for j in range(CHUNKS):
        o_load(j).start()

    def w_load(src, j, unit):
        slot = lax.rem(unit, SLOTS) if not isinstance(unit, int) else unit % SLOTS
        return local(
            src.at[:, cols(j)],
            wbuf.at[pl.ds(pl.multiple_of(slot * WIDTH, WIDTH), WIDTH), :],
            w_sem.at[slot],
        )

    for c in ins[:3]:
        c.wait()
    to = rgb[...]
    pick = lax.broadcasted_iota(jnp.int32, (ROWS, ROWS), 0) == lax.shift_right_logical(to, 7)
    pos = jnp.sum(
        jnp.where(pick, jnp.bitwise_and(to, 255).astype(F32), 0.0), axis=1, keepdims=True
    )
    pick = pick.astype(BF)
    pkv[:, :, KV_WIDTH:] = jnp.broadcast_to(pos, (ROWS, ROWS)).astype(BF).reshape(CHIPS, 2, ROWS)
    for j in range(KV_WIDTH // CHUNK):
        y_rows = jnp.dot(pick, kvl[:, cols(j)], preferred_element_type=F32).astype(BF)
        pkv[:, :, cols(j)] = y_rows.reshape(CHIPS, 2, CHUNK)

    pl.semaphore_wait(barrier, CHIPS)

    exchange = [
        remote(seg, segb.at[core], ex_send.at[0], ex_recv.at[0], sibling),
        remote(
            q.at[:, cols(other, HALF)], qb.at[rows_of(core), :], ex_send.at[1], ex_recv.at[1], sibling
        ),
        remote(
            k.at[:, cols(other, KV_HALF)], kb.at[rows_of(core), :], ex_send.at[2], ex_recv.at[2], sibling
        ),
        remote(
            v.at[:, cols(other, KV_HALF)], vb.at[rows_of(core), :], ex_send.at[3], ex_recv.at[3], sibling
        ),
    ]
    for c in exchange:
        c.start()

    def scatter(packets, landing, send, recv):
        here = local(packets.at[chip], landing.at[core, 0], recv.at[0])
        here.start()

        def one(i, there):
            group_of = i // PER_GROUP if isinstance(i, int) else lax.shift_right_logical(i, 3)
            remote(packets.at[there], landing.at[core, i], send, recv.at[group_of], (there, core)).start()

        each_chip(one)

    def scattered(packets, landing, send, recv):
        remote(
            packets.at[pl.ds(0, CHIPS - 1)], landing.at[core, pl.ds(0, CHIPS - 1)], send, recv.at[0], sibling
        ).wait_send()

    def group(i):
        return pl.ds(i * PER_GROUP, PER_GROUP)

    def forward(landing, i, send, recv):
        return remote(
            landing.at[core, group(i)], landing.at[core, group(i)], send.at[i], recv.at[i], sibling
        )

    def hand_on(landing, recv, send_f, recv_f):
        def one(i, c):
            block = landing.at[core, group(i)]
            local(block, block, recv.at[i]).wait()
            forward(landing, i, send_f, recv_f).start()
            return c

        lax.fori_loop(0, GROUPS, one, 0)

        def arrived(i, c):
            theirs = landing.at[other, group(i)]
            remote(theirs, theirs, send_f.at[i], recv_f.at[i], sibling).wait_recv()
            return c

        lax.fori_loop(0, GROUPS, arrived, 0)

    scatter(pkv, kvr, kv_send, kv_recv)

    for unit in range(2, SLOTS):
        w_load(gw if unit % 2 == 0 else uw, (unit - 2) // 2, unit).start()

    for c in ins[3:]:
        c.wait()
    for c in exchange:
        c.wait_recv()
    two = 2 * ROWS
    t_at = lax.broadcasted_iota(jnp.int32, (two, two), 0)
    s_at = lax.broadcasted_iota(jnp.int32, (two, two), 1)
    last = jnp.concatenate([segb[0], segb[1]], axis=1) - chip * two
    allowed = (s_at <= t_at) & (last >= t_at)
    for h in range(OWN_HEADS):
        own = pl.ds(h * HEAD, HEAD)
        key = pl.ds(h // 2 * HEAD, HEAD)
        raw = lax.dot_general(
            qb[:, own], kb[:, key], (((1,), (1,)), ((), ())), preferred_element_type=F32
        )
        scores = CAP * jnp.tanh(raw * (HEAD**-0.5 / CAP))
        probs = jnp.where(allowed, jnp.exp(scores), 0.0)
        totals = jnp.sum(probs, axis=-1, keepdims=True)
        mixed = jnp.dot(probs.astype(BF), vb[:, key], preferred_element_type=F32)
        att[:, own] = (mixed * (1.0 / totals)).astype(BF)

    def halves(landing, j, send, recv):
        return remote(
            part.at[rows_of(other), cols(j)], landing.at[:, cols(j)], send.at[j], recv.at[j], sibling
        )

    def project(j, c):
        o_load(j).wait()
        w = wbuf[pl.ds(pl.multiple_of(j * HALF, HALF), HALF), :]
        part[:, cols(j)] = jnp.dot(att[...], w, preferred_element_type=F32).astype(BF)
        halves(prec, j, pr_send, pr_recv).start()
        return c

    lax.fori_loop(0, CHUNKS, project, 0)
    w_load(gw, 4, SLOTS).start()
    w_load(uw, 4, SLOTS + 1).start()

    def sum_halves(j, squares):
        halves(prec, j, pr_send, pr_recv).wait_recv()
        both = part[rows_of(core), cols(j)].astype(F32) + prec[:, cols(j)].astype(F32)
        pf[:, cols(j)] = both
        return squares + lanes_sum(both * both)

    squares = lax.fori_loop(0, CHUNKS, sum_halves, jnp.zeros((ROWS, 128), F32))
    scale = lax.rsqrt(jnp.sum(squares, axis=-1, keepdims=True) * (1.0 / WIDTH) + EPS)

    def to_packets(j, c):
        stream = (rb[:, cols(j)].astype(F32) + pf[:, cols(j)] * scale * ag_row[cols(j)].reshape(1, CHUNK)).astype(BF)
        y_rows = jnp.dot(pick, stream, preferred_element_type=F32).astype(BF)
        pks[:, :, cols(j)] = y_rows.reshape(CHIPS, 2, CHUNK)
        return c

    lax.fori_loop(0, CHUNKS, to_packets, 0)
    scatter(pks, strr, st_send, st_recv)

    hand_on(kvr, kv_recv, kvf_send, kvf_recv)
    at = kvr[:, :, :, KV_WIDTH:].reshape(two, 128).astype(F32)
    at = jnp.transpose(at)[0:1, :].astype(jnp.int32)
    place = (t_at == at).astype(BF)
    own_place = (t_at[0:ROWS, :] + core * ROWS == at).astype(BF)
    for j in range(KV_WIDTH // CHUNK):
        got = jnp.dot(
            own_place, kvr[:, :, :, cols(j)].reshape(two, CHUNK), preferred_element_type=F32
        ).astype(BF)
        kvb[2 * j] = got[:, 0:HEAD]
        kvb[2 * j + 1] = got[:, HEAD:]
    outs = [local(kvb, kvo, out_sem.at[0])]
    outs[0].start()

    hand_on(strr, st_recv, stf_send, stf_recv)

    def put(j, squares):
        got = jnp.dot(
            place, strr[:, :, :, cols(j)].reshape(two, CHUNK), preferred_element_type=F32
        )
        pb[:, cols(j)] = got.astype(BF)
        return squares + lanes_sum(got * got)

    squares = lax.fori_loop(0, CHUNKS, put, jnp.zeros((two, 128), F32))
    scale = lax.rsqrt(jnp.sum(squares, axis=-1, keepdims=True) * (1.0 / WIDTH) + EPS)

    def norm(j, c):
        xb[:, cols(j)] = (pb[:, cols(j)].astype(F32) * scale * pg_row[cols(j)].reshape(1, CHUNK)).astype(BF)
        return c

    lax.fori_loop(0, CHUNKS, norm, 0)
    outs.append(local(pb.at[rows_of(core), :], own_rows, out_sem.at[1]))
    outs[1].start()

    def weight(unit, i):
        slot = lax.rem(unit, SLOTS)
        return wbuf[
            pl.ds(pl.multiple_of(slot * WIDTH, WIDTH), WIDTH), pl.ds(i * 256, 256)
        ]

    def loaded(unit):
        slot = lax.rem(unit, SLOTS)
        block = wbuf.at[pl.ds(pl.multiple_of(slot * WIDTH, WIDTH), WIDTH), :]
        local(block, block, w_sem.at[slot]).wait()

    def hidden(j, c):
        loaded(2 + 2 * j)
        loaded(3 + 2 * j)
        for i in range(CHUNK // 256):
            u = jnp.dot(xb[...], weight(2 + 2 * j, i), preferred_element_type=F32)
            up = jnp.dot(xb[...], weight(3 + 2 * j, i), preferred_element_type=F32)
            gelu = 0.5 * u * (1.0 + jnp.tanh(0.7978845608028654 * (u + 0.044715 * (u * u * u))))
            act[:, pl.ds(pl.multiple_of(j * CHUNK + i * 256, 256), 256)] = (gelu * up).astype(BF)

        @pl.when(j < 2)
        def _():
            w_load(gw, 5 + j, 12 + 2 * j).start()
            w_load(uw, 5 + j, 13 + 2 * j).start()

        @pl.when((j >= 2) & (j < 6))
        def _():
            w_load(dw, 2 * (j - 2), 12 + 2 * j).start()

        @pl.when((j >= 2) & (j < 5))
        def _():
            w_load(dw, 2 * (j - 2) + 1, 13 + 2 * j).start()

        return c

    lax.fori_loop(0, CHUNKS, hidden, 0)

    def projected(j, c):
        halves(prec, j, pr_send, pr_recv).wait_send()
        return c

    lax.fori_loop(0, CHUNKS, projected, 0)

    def kept(j):
        return local(part.at[rows_of(core), cols(j)], mine.at[:, cols(j)], keep_sem.at[j])

    def down(j, c):
        loaded(16 + j)
        for i in range(CHUNK // 256):
            got = jnp.dot(act[...], weight(16 + j, i), preferred_element_type=F32)
            part[:, pl.ds(pl.multiple_of(j * CHUNK + i * 256, 256), 256)] = got.astype(BF)
        halves(theirs, j, dn_send, dn_recv).start()
        kept(j).start()
        return c

    lax.fori_loop(0, CHUNKS, down, 0)

    for c in exchange:
        c.wait_send()
    scattered(pkv, kvr, kv_send, kv_recv)
    scattered(pks, strr, st_send, st_recv)

    def sent(i, c):
        forward(kvr, i, kvf_send, kvf_recv).wait_send()
        forward(strr, i, stf_send, stf_recv).wait_send()
        return c

    lax.fori_loop(0, GROUPS, sent, 0)

    def down_sent(j, c):
        halves(theirs, j, dn_send, dn_recv).wait()
        kept(j).wait()
        return c

    lax.fori_loop(0, CHUNKS, down_sent, 0)
    for c in outs:
        c.wait()


def last(mine, theirs, own_rows, kvo, og, lo, kc, vc, mb, tb, ob, kvb, og_row, in_sem, kv_sem, og_sem, out_sem):
    def copy(src, dst, sem):
        return pltpu.make_async_copy(src, dst, sem)

    pairs = ((mine, mb), (theirs, tb), (own_rows, ob))

    def load(n, j):
        src, dst = pairs[n]
        return copy(src.at[:, cols(j)], dst.at[:, cols(j)], in_sem.at[n, j])

    for j in range(CHUNKS):
        load(0, j).start()
        load(1, j).start()
    gain = copy(og, og_row, og_sem)
    gain.start()
    for j in range(CHUNKS):
        load(2, j).start()
    caches = [
        copy(kvo.at[pl.ds(0, 4)], kvb.at[pl.ds(0, 4)], kv_sem.at[0]),
        copy(kvo.at[pl.ds(4, 4)], kvb.at[pl.ds(4, 4)], kv_sem.at[1]),
    ]
    for c in caches:
        c.start()
    squares = jnp.zeros((ROWS, 128), F32)
    for j in range(CHUNKS):
        load(0, j).wait()
        load(1, j).wait()
        both = mb[:, cols(j)].astype(F32) + tb[:, cols(j)].astype(F32)
        squares = squares + lanes_sum(both * both)
    for c in caches:
        c.wait()
    caches = [
        copy(kvb.at[pl.ds(0, 4)], kc, kv_sem.at[0]),
        copy(kvb.at[pl.ds(4, 4)], vc, kv_sem.at[1]),
    ]
    for c in caches:
        c.start()
    scale = lax.rsqrt(jnp.sum(squares, axis=-1, keepdims=True) * (1.0 / WIDTH) + EPS)
    gain.wait()

    def store(j):
        return copy(mb.at[:, cols(j)], lo.at[:, cols(j)], out_sem.at[j])

    for j in range(CHUNKS):
        load(2, j).wait()
        both = mb[:, cols(j)].astype(F32) + tb[:, cols(j)].astype(F32)
        row = og_row[cols(j)].reshape(1, CHUNK)
        mb[:, cols(j)] = (ob[:, cols(j)].astype(F32) + both * scale * row).astype(BF)
        store(j).start()
    for j in range(CHUNKS):
        store(j).wait()
    for c in caches:
        c.wait()


def per_device(
    queries,
    keys,
    values,
    residual,
    segment_ids,
    regroup,
    out_weight,
    attn_gain,
    pre_gain,
    gate_weight,
    up_weight,
    down_weight,
    post_gain,
):
    dma = pltpu.SemaphoreType.DMA
    vmem = pltpu.VMEM
    mine, theirs, own_rows, kvo = pl.pallas_call(
        kernel,
        out_shape=(
            jax.ShapeDtypeStruct((ROWS, WIDTH), BF),
            jax.ShapeDtypeStruct((ROWS, WIDTH), BF),
            jax.ShapeDtypeStruct((ROWS, WIDTH), BF),
            jax.ShapeDtypeStruct((8, ROWS, HEAD), BF),
        ),
        in_specs=[pl.BlockSpec(memory_space=pl.ANY)] * 12,
        out_specs=(pl.BlockSpec(memory_space=pl.ANY),) * 4,
        scratch_shapes=[
            vmem((SLOTS * WIDTH, CHUNK), BF),
            vmem((2 * ROWS, HALF), BF),
            vmem((2 * ROWS, KV_HALF), BF),
            vmem((2 * ROWS, KV_HALF), BF),
            vmem((2, 1, ROWS), jnp.int32),
            vmem((ROWS, KV_WIDTH), BF),
            vmem((1, ROWS), jnp.int32),
            vmem((WIDTH,), F32),
            vmem((WIDTH,), F32),
            vmem((ROWS, WIDTH), BF),
            vmem((2 * ROWS, HALF), BF),
            vmem((2 * ROWS, WIDTH), BF),
            vmem((ROWS, WIDTH), BF),
            vmem((CHIPS, 2, KV_WIDTH + 128), BF),
            vmem((2, CHIPS, 2, KV_WIDTH + 128), BF),
            vmem((CHIPS, 2, WIDTH), BF),
            vmem((2, CHIPS, 2, WIDTH), BF),
            vmem((2 * ROWS, WIDTH), BF),
            vmem((2 * ROWS, WIDTH), BF),
            vmem((2 * ROWS, WIDTH), BF),
            vmem((8, ROWS, HEAD), BF),
            vmem((ROWS, WIDTH), F32),
            dma((10,)),
            dma((CHUNKS,)),
            dma((SLOTS,)),
            dma((2,)),
            dma((CHUNKS,)),
            dma((4,)),
            dma((4,)),
            dma((CHUNKS,)),
            dma((CHUNKS,)),
            dma((CHUNKS,)),
            dma((CHUNKS,)),
            dma,
            dma((GROUPS,)),
            dma((GROUPS,)),
            dma((GROUPS,)),
            dma,
            dma((GROUPS,)),
            dma((GROUPS,)),
            dma((GROUPS,)),
        ],
        compiler_params=pltpu.CompilerParams(
            collective_id=0, has_side_effects=True, vmem_limit_bytes=62 * 1024 * 1024
        ),
        name="layer",
    )(
        queries,
        keys,
        values,
        residual,
        segment_ids.reshape(1, ROWS),
        regroup.reshape(1, ROWS),
        out_weight,
        attn_gain,
        pre_gain,
        gate_weight,
        up_weight,
        down_weight,
    )
    return pl.pallas_call(
        last,
        out_shape=(
            jax.ShapeDtypeStruct((ROWS, WIDTH), BF),
            jax.ShapeDtypeStruct((4, ROWS, HEAD), BF),
            jax.ShapeDtypeStruct((4, ROWS, HEAD), BF),
        ),
        in_specs=[pl.BlockSpec(memory_space=pl.ANY)] * 5,
        out_specs=(pl.BlockSpec(memory_space=pl.ANY),) * 3,
        scratch_shapes=[
            vmem((ROWS, WIDTH), BF),
            vmem((ROWS, WIDTH), BF),
            vmem((ROWS, WIDTH), BF),
            vmem((8, ROWS, HEAD), BF),
            vmem((WIDTH,), F32),
            dma((3, CHUNKS)),
            dma((2,)),
            dma,
            dma((CHUNKS,)),
        ],
        compiler_params=pltpu.CompilerParams(vmem_limit_bytes=62 * 1024 * 1024),
        name="last",
    )(mine, theirs, own_rows, kvo, post_gain)


def solution(mesh):
    rows = P(("req", "kv"), None)
    flat = P(("req", "kv"))
    return jax.shard_map(
        per_device,
        mesh=mesh,
        in_specs=(
            rows, rows, rows, rows, flat, flat, P("kv", None), P(), P(),
            P(None, "kv"), P(None, "kv"), P("kv", None), P(),
        ),
        out_specs=(rows, P(None, ("req", "kv"), None), P(None, ("req", "kv"), None)),
        check_vma=False,
    )
```

```python
import jax
import jax.numpy as jnp
from jax import lax
from jax.experimental import pallas as pl
from jax.experimental.pallas import tpu as pltpu
from jax.sharding import PartitionSpec as P

MESH = pl.DeviceIdType.MESH
CHIPS = 64
SIDE = 4
ROWS = 128
WIDTH = 3584
HEAD = 256
OWN_HEADS = 4
HALF = 1024
KV_HALF = 512
KV_WIDTH = 2048
CHUNK = 512
CHUNKS = WIDTH // CHUNK
FIRST = 3
SECOND = CHUNKS - FIRST
A_ROWS = FIRST * CHUNK
B_ROWS = SECOND * CHUNK
UNITS = 2 * CHUNKS
B_SLOTS = 8
B_BASE = UNITS * A_ROWS
GROUPS = 8
PER_GROUP = CHIPS // GROUPS
CAP = 50.0
EPS = 1e-06
BF = jnp.bfloat16
F32 = jnp.float32


def cols(j, width=CHUNK):
    if isinstance(j, int):
        return pl.ds(j * width, width)
    return pl.ds(pl.multiple_of(j * width, width), width)


def rows_of(core):
    return pl.ds(pl.multiple_of(core * ROWS, ROWS), ROWS)


def lanes_sum(value):
    total = value[:, 0:128]
    for i in range(1, CHUNK // 128):
        total = total + value[:, i * 128 : (i + 1) * 128]
    return total


def kernel(
    q, k, v, res, seg, rg, ow, ag, pg, gw, uw, dw,
    mine, theirs, own_rows, kvo,
    wbuf, qb, kb, vb, segb, kvl, rgb, ag_row, pg_row, rb, att, part, prec, pkv, kvr, pka, pkb, sta, stb,
    xb, act, kvb, gacc, uacc,
    in_sem, o_sem, a_sem, b_sem, d_sem, out_sem, keep_sem, ex_send, ex_recv, pr_send, pr_recv, dn_send, dn_recv,
    kv_send, kv_recv, kvf_send, kvf_recv,
    sa_send, sa_recv, saf_send, saf_recv, sb_send, sb_recv, sbf_send, sbf_recv,
):
    chip = lax.axis_index("req")
    core = lax.axis_index("kv")
    other = 1 - core
    sibling = (chip, other)
    z = lax.div(chip, SIDE * SIDE)
    plane = chip - z * (SIDE * SIDE)
    y = lax.div(plane, SIDE)
    x = plane - y * SIDE

    def wrap(at):
        return jnp.where(at >= SIDE, at - SIDE, at)

    across = [wrap(x + n) for n in range(SIDE)]

    def each_chip(do):
        def outer(a, za):
            def inner(b, yb):
                for n in range(SIDE):
                    there = wrap(za + n) * (SIDE * SIDE) + wrap(yb + n) * SIDE + across[n]
                    if n == 0:

                        @pl.when(a + b > 0)
                        def _():
                            do(a * (SIDE * SIDE) + b * SIDE, there)
                    else:
                        do(a * (SIDE * SIDE) + b * SIDE + n, there)
                return wrap(yb + 1)

            lax.fori_loop(0, SIDE, inner, y)
            return wrap(za + 1)

        lax.fori_loop(0, SIDE, outer, z)

    def local(src, dst, sem):
        return pltpu.make_async_copy(src, dst, sem)

    def remote(src, dst, send, recv, device):
        return pltpu.make_async_remote_copy(
            src_ref=src, dst_ref=dst, send_sem=send, recv_sem=recv, device_id=device, device_id_type=MESH
        )

    barrier = pltpu.get_barrier_semaphore()
    pl.semaphore_signal(barrier, inc=1, device_id=sibling, device_id_type=MESH)

    def greet(i, there):
        pl.semaphore_signal(barrier, inc=1, device_id=(there, core), device_id_type=MESH)

    each_chip(greet)

    ins = [
        local(rg, rgb, in_sem.at[0]),
        local(k, kvl.at[:, pl.ds(0, HALF)], in_sem.at[1]),
        local(v, kvl.at[:, pl.ds(HALF, HALF)], in_sem.at[2]),
        local(seg, segb.at[core], in_sem.at[3]),
        local(q.at[:, cols(core, HALF)], qb.at[rows_of(core), :], in_sem.at[4]),
        local(k.at[:, cols(core, KV_HALF)], kb.at[rows_of(core), :], in_sem.at[5]),
        local(v.at[:, cols(core, KV_HALF)], vb.at[rows_of(core), :], in_sem.at[6]),
        local(ag, ag_row, in_sem.at[7]),
        local(pg, pg_row, in_sem.at[8]),
        local(res, rb, in_sem.at[9]),
    ]
    for c in ins:
        c.start()

    def wrows(start, count):
        return wbuf.at[pl.ds(pl.multiple_of(start, CHUNK), count), :]

    def o_load(j):
        return local(ow.at[:, cols(j)], wrows(B_BASE + j * HALF, HALF), o_sem.at[j])

    for j in range(CHUNKS):
        o_load(j).start()

    def a_load(src, j, unit):
        return local(src.at[pl.ds(0, A_ROWS), cols(j)], wrows(unit * A_ROWS, A_ROWS), a_sem.at[unit])

    def b_start(unit):
        return B_BASE + lax.rem(unit, B_SLOTS) * B_ROWS

    def b_load(src, j, unit):
        return local(src.at[pl.ds(A_ROWS, B_ROWS), cols(j)], wrows(b_start(unit), B_ROWS), b_sem.at[unit])

    def d_start(j):
        return jnp.where(j < CHUNKS - 1, j * WIDTH, B_BASE + 6 * B_ROWS)

    def d_load(j):
        return local(dw.at[:, cols(j)], wrows(d_start(j), WIDTH), d_sem.at[j])

    for c in ins[:3]:
        c.wait()
    to = rgb[...]
    pick = lax.broadcasted_iota(jnp.int32, (ROWS, ROWS), 0) == lax.shift_right_logical(to, 7)
    pos = jnp.sum(
        jnp.where(pick, jnp.bitwise_and(to, 255).astype(F32), 0.0), axis=1, keepdims=True
    )
    pick = pick.astype(BF)
    pkv[:, :, KV_WIDTH:] = jnp.broadcast_to(pos, (ROWS, ROWS)).astype(BF).reshape(CHIPS, 2, ROWS)
    for j in range(KV_WIDTH // CHUNK):
        y_rows = jnp.dot(pick, kvl[:, cols(j)], preferred_element_type=F32).astype(BF)
        pkv[:, :, cols(j)] = y_rows.reshape(CHIPS, 2, CHUNK)

    pl.semaphore_wait(barrier, CHIPS)

    exchange = [
        remote(seg, segb.at[core], ex_send.at[0], ex_recv.at[0], sibling),
        remote(
            q.at[:, cols(other, HALF)], qb.at[rows_of(core), :], ex_send.at[1], ex_recv.at[1], sibling
        ),
        remote(
            k.at[:, cols(other, KV_HALF)], kb.at[rows_of(core), :], ex_send.at[2], ex_recv.at[2], sibling
        ),
        remote(
            v.at[:, cols(other, KV_HALF)], vb.at[rows_of(core), :], ex_send.at[3], ex_recv.at[3], sibling
        ),
    ]
    for c in exchange:
        c.start()

    def scatter(packets, landing, send, recv):
        here = local(packets.at[chip], landing.at[core, 0], recv.at[0])
        here.start()

        def one(i, there):
            group_of = i // PER_GROUP if isinstance(i, int) else lax.shift_right_logical(i, 3)
            remote(packets.at[there], landing.at[core, i], send, recv.at[group_of], (there, core)).start()

        each_chip(one)

    def scattered(packets, landing, send, recv):
        remote(
            packets.at[pl.ds(0, CHIPS - 1)], landing.at[core, pl.ds(0, CHIPS - 1)], send, recv.at[0], sibling
        ).wait_send()

    def group(i):
        return pl.ds(i * PER_GROUP, PER_GROUP)

    def forward(landing, i, send, recv):
        return remote(
            landing.at[core, group(i)], landing.at[core, group(i)], send.at[i], recv.at[i], sibling
        )

    def hand_on(landing, i, recv, send_f, recv_f):
        block = landing.at[core, group(i)]
        local(block, block, recv.at[i]).wait()
        forward(landing, i, send_f, recv_f).start()

    def arrive(landing, send_f, recv_f):
        def one(i, c):
            theirs = landing.at[other, group(i)]
            remote(theirs, theirs, send_f.at[i], recv_f.at[i], sibling).wait_recv()
            return c

        lax.fori_loop(0, GROUPS, one, 0)

    def hand_on_all(landing, recv, send_f, recv_f):
        def one(i, c):
            hand_on(landing, i, recv, send_f, recv_f)
            return c

        lax.fori_loop(0, GROUPS, one, 0)
        arrive(landing, send_f, recv_f)

    scatter(pkv, kvr, kv_send, kv_recv)

    for unit in range(UNITS):
        a_load((gw, uw)[unit % 2], unit // 2, unit).start()
    for unit in range(4, B_SLOTS):
        b_load((gw, uw)[unit % 2], unit // 2, unit).start()

    for c in ins[3:]:
        c.wait()
    for c in exchange:
        c.wait_recv()
    two = 2 * ROWS
    t_at = lax.broadcasted_iota(jnp.int32, (two, two), 0)
    s_at = lax.broadcasted_iota(jnp.int32, (two, two), 1)
    last = jnp.concatenate([segb[0], segb[1]], axis=1) - chip * two
    allowed = (s_at <= t_at) & (last >= t_at)
    for h in range(OWN_HEADS):
        own = pl.ds(h * HEAD, HEAD)
        key = pl.ds(h // 2 * HEAD, HEAD)
        raw = lax.dot_general(
            qb[:, own], kb[:, key], (((1,), (1,)), ((), ())), preferred_element_type=F32
        )
        scores = CAP * jnp.tanh(raw * (HEAD**-0.5 / CAP))
        probs = jnp.where(allowed, jnp.exp(scores), 0.0)
        totals = jnp.sum(probs, axis=-1, keepdims=True)
        mixed = jnp.dot(probs.astype(BF), vb[:, key], preferred_element_type=F32)
        att[:, own] = (mixed * (1.0 / totals)).astype(BF)

    def halves(landing, j, send, recv):
        return remote(
            part.at[rows_of(other), cols(j)], landing.at[:, cols(j)], send.at[j], recv.at[j], sibling
        )

    def project(j, c):
        o_load(j).wait()
        w = wrows(B_BASE + j * HALF, HALF)[...]
        part[:, cols(j)] = jnp.dot(att[...], w, preferred_element_type=F32).astype(BF)
        halves(prec, j, pr_send, pr_recv).start()
        return c

    lax.fori_loop(0, CHUNKS, project, 0)
    for unit in range(4):
        b_load((gw, uw)[unit % 2], unit // 2, unit).start()

    def sum_halves(j, squares):
        halves(prec, j, pr_send, pr_recv).wait_recv()
        both = part[rows_of(core), cols(j)].astype(F32) + prec[:, cols(j)].astype(F32)
        gacc[0:ROWS, cols(j)] = both
        return squares + lanes_sum(both * both)

    squares = lax.fori_loop(0, CHUNKS, sum_halves, jnp.zeros((ROWS, 128), F32))
    scale = lax.rsqrt(jnp.sum(squares, axis=-1, keepdims=True) * (1.0 / WIDTH) + EPS)

    def to_packets(packets, first):
        def one(j, c):
            at = cols(first + j)
            added = gacc[0:ROWS, at] * scale * ag_row[at].reshape(1, CHUNK)
            stream = (rb[:, at].astype(F32) + added).astype(BF)
            y_rows = jnp.dot(pick, stream, preferred_element_type=F32).astype(BF)
            packets[:, :, cols(j)] = y_rows.reshape(CHIPS, 2, CHUNK)
            return c

        return one

    lax.fori_loop(0, FIRST, to_packets(pka, 0), 0)
    scatter(pka, sta, sa_send, sa_recv)
    lax.fori_loop(0, SECOND, to_packets(pkb, FIRST), 0)
    scatter(pkb, stb, sb_send, sb_recv)

    hand_on_all(kvr, kv_recv, kvf_send, kvf_recv)
    at = kvr[:, :, :, KV_WIDTH:].reshape(two, 128).astype(F32)
    at = jnp.transpose(at)[0:1, :].astype(jnp.int32)
    place = (t_at == at).astype(BF)
    own_place = (t_at[0:ROWS, :] + core * ROWS == at).astype(BF)
    for j in range(KV_WIDTH // CHUNK):
        got = jnp.dot(
            own_place, kvr[:, :, :, cols(j)].reshape(two, CHUNK), preferred_element_type=F32
        ).astype(BF)
        kvb[2 * j] = got[:, 0:HEAD]
        kvb[2 * j + 1] = got[:, HEAD:]
    outs = [local(kvb, kvo, out_sem.at[0])]
    outs[0].start()

    def put(landing, first):
        def one(j, squares):
            rows = landing[:, :, :, cols(j)].reshape(two, CHUNK)
            got = jnp.dot(place, rows, preferred_element_type=F32)
            at = cols(first + j)
            xb[:, at] = (got * pg_row[at].reshape(1, CHUNK)).astype(BF)
            rb[:, at] = jnp.dot(own_place, rows, preferred_element_type=F32).astype(BF)
            return squares + lanes_sum(got * got)

        return one

    hand_on_all(sta, sa_recv, saf_send, saf_recv)
    squares = lax.fori_loop(0, FIRST, put(sta, 0), jnp.zeros((two, 128), F32))

    def product(first, depth, start, i):
        w = wbuf[pl.ds(pl.multiple_of(start, CHUNK), depth), pl.ds(i * 256, 256)]
        return jnp.dot(xb[:, pl.ds(first, depth)], w, preferred_element_type=F32)

    def at256(j, i):
        return pl.ds(pl.multiple_of(j * CHUNK + i * 256, 256), 256)

    def begin(j, c):
        for m in range(2):
            a_load(gw, j, 2 * j + m).wait()
        for i in range(CHUNK // 256):
            gacc[:, at256(j, i)] = product(0, A_ROWS, 2 * j * A_ROWS, i)
            uacc[:, at256(j, i)] = product(0, A_ROWS, (2 * j + 1) * A_ROWS, i)

        @pl.when(j > 0)
        def _():
            d_load(j - 1).start()

        hand_on(stb, j, sb_recv, sbf_send, sbf_recv)
        return c

    lax.fori_loop(0, CHUNKS, begin, 0)
    hand_on(stb, CHUNKS, sb_recv, sbf_send, sbf_recv)
    arrive(stb, sbf_send, sbf_recv)
    squares = lax.fori_loop(0, SECOND, put(stb, FIRST), squares)
    scale = lax.rsqrt(jnp.sum(squares, axis=-1, keepdims=True) * (1.0 / WIDTH) + EPS)
    outs.append(local(rb, own_rows, out_sem.at[1]))
    outs[1].start()

    def hidden(j, c):
        for m in range(2):
            b_load(gw, j, 2 * j + m).wait()
        for i in range(CHUNK // 256):
            at = at256(j, i)
            u = (gacc[:, at] + product(A_ROWS, B_ROWS, b_start(2 * j), i)) * scale
            up = (uacc[:, at] + product(A_ROWS, B_ROWS, b_start(2 * j + 1), i)) * scale
            gelu = 0.5 * u * (1.0 + jnp.tanh(0.7978845608028654 * (u + 0.044715 * (u * u * u))))
            act[:, at] = (gelu * up).astype(BF)

        @pl.when(j < CHUNKS - B_SLOTS // 2)
        def _():
            b_load(gw, j + B_SLOTS // 2, 2 * j + B_SLOTS).start()
            b_load(uw, j + B_SLOTS // 2, 2 * j + 1 + B_SLOTS).start()

        @pl.when(j == CHUNKS - B_SLOTS // 2)
        def _():
            d_load(CHUNKS - 1).start()

        return c

    lax.fori_loop(0, CHUNKS, hidden, 0)

    def projected(j, c):
        halves(prec, j, pr_send, pr_recv).wait_send()
        return c

    lax.fori_loop(0, CHUNKS, projected, 0)

    def kept(j):
        return local(part.at[rows_of(core), cols(j)], mine.at[:, cols(j)], keep_sem.at[j])

    def down(j, c):
        d_load(j).wait()
        for i in range(CHUNK // 256):
            w = wbuf[pl.ds(pl.multiple_of(d_start(j), CHUNK), WIDTH), pl.ds(i * 256, 256)]
            part[:, at256(j, i)] = jnp.dot(act[...], w, preferred_element_type=F32).astype(BF)
        halves(theirs, j, dn_send, dn_recv).start()
        kept(j).start()
        return c

    lax.fori_loop(0, CHUNKS, down, 0)

    for c in exchange:
        c.wait_send()
    scattered(pkv, kvr, kv_send, kv_recv)
    scattered(pka, sta, sa_send, sa_recv)
    scattered(pkb, stb, sb_send, sb_recv)

    def sent(i, c):
        forward(kvr, i, kvf_send, kvf_recv).wait_send()
        forward(sta, i, saf_send, saf_recv).wait_send()
        forward(stb, i, sbf_send, sbf_recv).wait_send()
        return c

    lax.fori_loop(0, GROUPS, sent, 0)

    def down_sent(j, c):
        halves(theirs, j, dn_send, dn_recv).wait()
        kept(j).wait()
        return c

    lax.fori_loop(0, CHUNKS, down_sent, 0)
    for c in outs:
        c.wait()


def last(mine, theirs, own_rows, kvo, og, lo, kc, vc, mb, tb, ob, kvb, og_row, in_sem, kv_sem, og_sem, out_sem):
    def copy(src, dst, sem):
        return pltpu.make_async_copy(src, dst, sem)

    pairs = ((mine, mb), (theirs, tb), (own_rows, ob))

    def load(n, j):
        src, dst = pairs[n]
        return copy(src.at[:, cols(j)], dst.at[:, cols(j)], in_sem.at[n, j])

    for j in range(CHUNKS):
        load(0, j).start()
        load(1, j).start()
    gain = copy(og, og_row, og_sem)
    gain.start()
    for j in range(CHUNKS):
        load(2, j).start()
    caches = [
        copy(kvo.at[pl.ds(0, 4)], kvb.at[pl.ds(0, 4)], kv_sem.at[0]),
        copy(kvo.at[pl.ds(4, 4)], kvb.at[pl.ds(4, 4)], kv_sem.at[1]),
    ]
    for c in caches:
        c.start()
    squares = jnp.zeros((ROWS, 128), F32)
    for j in range(CHUNKS):
        load(0, j).wait()
        load(1, j).wait()
        both = mb[:, cols(j)].astype(F32) + tb[:, cols(j)].astype(F32)
        squares = squares + lanes_sum(both * both)
    for c in caches:
        c.wait()
    caches = [
        copy(kvb.at[pl.ds(0, 4)], kc, kv_sem.at[0]),
        copy(kvb.at[pl.ds(4, 4)], vc, kv_sem.at[1]),
    ]
    for c in caches:
        c.start()
    scale = lax.rsqrt(jnp.sum(squares, axis=-1, keepdims=True) * (1.0 / WIDTH) + EPS)
    gain.wait()

    def store(j):
        return copy(mb.at[:, cols(j)], lo.at[:, cols(j)], out_sem.at[j])

    for j in range(CHUNKS):
        load(2, j).wait()
        both = mb[:, cols(j)].astype(F32) + tb[:, cols(j)].astype(F32)
        row = og_row[cols(j)].reshape(1, CHUNK)
        mb[:, cols(j)] = (ob[:, cols(j)].astype(F32) + both * scale * row).astype(BF)
        store(j).start()
    for j in range(CHUNKS):
        store(j).wait()
    for c in caches:
        c.wait()


def per_device(
    queries,
    keys,
    values,
    residual,
    segment_ids,
    regroup,
    out_weight,
    attn_gain,
    pre_gain,
    gate_weight,
    up_weight,
    down_weight,
    post_gain,
):
    dma = pltpu.SemaphoreType.DMA
    vmem = pltpu.VMEM
    mine, theirs, own_rows, kvo = pl.pallas_call(
        kernel,
        out_shape=(
            jax.ShapeDtypeStruct((ROWS, WIDTH), BF),
            jax.ShapeDtypeStruct((ROWS, WIDTH), BF),
            jax.ShapeDtypeStruct((ROWS, WIDTH), BF),
            jax.ShapeDtypeStruct((8, ROWS, HEAD), BF),
        ),
        in_specs=[pl.BlockSpec(memory_space=pl.ANY)] * 12,
        out_specs=(pl.BlockSpec(memory_space=pl.ANY),) * 4,
        scratch_shapes=[
            vmem((B_BASE + B_SLOTS * B_ROWS, CHUNK), BF),
            vmem((2 * ROWS, HALF), BF),
            vmem((2 * ROWS, KV_HALF), BF),
            vmem((2 * ROWS, KV_HALF), BF),
            vmem((2, 1, ROWS), jnp.int32),
            vmem((ROWS, KV_WIDTH), BF),
            vmem((1, ROWS), jnp.int32),
            vmem((WIDTH,), F32),
            vmem((WIDTH,), F32),
            vmem((ROWS, WIDTH), BF),
            vmem((2 * ROWS, HALF), BF),
            vmem((2 * ROWS, WIDTH), BF),
            vmem((ROWS, WIDTH), BF),
            vmem((CHIPS, 2, KV_WIDTH + 128), BF),
            vmem((2, CHIPS, 2, KV_WIDTH + 128), BF),
            vmem((CHIPS, 2, A_ROWS), BF),
            vmem((CHIPS, 2, B_ROWS), BF),
            vmem((2, CHIPS, 2, A_ROWS), BF),
            vmem((2, CHIPS, 2, B_ROWS), BF),
            vmem((2 * ROWS, WIDTH), BF),
            vmem((2 * ROWS, WIDTH), BF),
            vmem((8, ROWS, HEAD), BF),
            vmem((2 * ROWS, WIDTH), F32),
            vmem((2 * ROWS, WIDTH), F32),
            dma((10,)),
            dma((CHUNKS,)),
            dma((UNITS,)),
            dma((UNITS,)),
            dma((CHUNKS,)),
            dma((2,)),
            dma((CHUNKS,)),
            dma((4,)),
            dma((4,)),
            dma((CHUNKS,)),
            dma((CHUNKS,)),
            dma((CHUNKS,)),
            dma((CHUNKS,)),
            *[dma, dma((GROUPS,)), dma((GROUPS,)), dma((GROUPS,))] * 3,
        ],
        compiler_params=pltpu.CompilerParams(
            collective_id=0, has_side_effects=True, vmem_limit_bytes=62 * 1024 * 1024
        ),
        name="layer",
    )(
        queries,
        keys,
        values,
        residual,
        segment_ids.reshape(1, ROWS),
        regroup.reshape(1, ROWS),
        out_weight,
        attn_gain,
        pre_gain,
        gate_weight,
        up_weight,
        down_weight,
    )
    return pl.pallas_call(
        last,
        out_shape=(
            jax.ShapeDtypeStruct((ROWS, WIDTH), BF),
            jax.ShapeDtypeStruct((4, ROWS, HEAD), BF),
            jax.ShapeDtypeStruct((4, ROWS, HEAD), BF),
        ),
        in_specs=[pl.BlockSpec(memory_space=pl.ANY)] * 5,
        out_specs=(pl.BlockSpec(memory_space=pl.ANY),) * 3,
        scratch_shapes=[
            vmem((ROWS, WIDTH), BF),
            vmem((ROWS, WIDTH), BF),
            vmem((ROWS, WIDTH), BF),
            vmem((8, ROWS, HEAD), BF),
            vmem((WIDTH,), F32),
            dma((3, CHUNKS)),
            dma((2,)),
            dma,
            dma((CHUNKS,)),
        ],
        compiler_params=pltpu.CompilerParams(vmem_limit_bytes=62 * 1024 * 1024),
        name="last",
    )(mine, theirs, own_rows, kvo, post_gain)


def solution(mesh):
    rows = P(("req", "kv"), None)
    flat = P(("req", "kv"))
    return jax.shard_map(
        per_device,
        mesh=mesh,
        in_specs=(
            rows, rows, rows, rows, flat, flat, P("kv", None), P(), P(),
            P(None, "kv"), P(None, "kv"), P("kv", None), P(),
        ),
        out_specs=(rows, P(None, ("req", "kv"), None), P(None, ("req", "kv"), None)),
        check_vma=False,
    )
```

```python
import jax
import jax.numpy as jnp
from jax import lax
from jax.experimental import pallas as pl
from jax.experimental.pallas import tpu as pltpu
from jax.sharding import PartitionSpec as P

MESH = pl.DeviceIdType.MESH
CHIPS = 64
SIDE = 4
ROWS = 128
WIDTH = 3584
HEAD = 256
OWN_HEADS = 4
HALF = 1024
KV_HALF = 512
KV_WIDTH = 2048
CHUNK = 512
CHUNKS = WIDTH // CHUNK
FIRST = 3
SECOND = CHUNKS - FIRST
A_ROWS = FIRST * CHUNK
B_ROWS = SECOND * CHUNK
UNITS = 2 * CHUNKS
B_SLOTS = 8
B_BASE = UNITS * A_ROWS
GROUPS = 8
PER_GROUP = CHIPS // GROUPS
CAP = 50.0
EPS = 1e-06
BF = jnp.bfloat16
F32 = jnp.float32


def cols(j, width=CHUNK):
    if isinstance(j, int):
        return pl.ds(j * width, width)
    return pl.ds(pl.multiple_of(j * width, width), width)


def rows_of(core):
    return pl.ds(pl.multiple_of(core * ROWS, ROWS), ROWS)


def lanes_sum(value):
    total = value[:, 0:128]
    for i in range(1, CHUNK // 128):
        total = total + value[:, i * 128 : (i + 1) * 128]
    return total


def kernel(
    q, k, v, res, seg, rg, ow, ag, pg, gw, uw, dw,
    mine, theirs, own_rows, kvo,
    wbuf, qb, kb, vb, segb, kvl, rgb, ag_row, pg_row, rb, att, part, prec, pkv, kvr, pka, pkb, sta, stb,
    xb, act, gacc, uacc,
    in_sem, o_sem, a_sem, b_sem, d_sem, keep_sem, ex_send, ex_recv, pr_send, pr_recv, dn_send, dn_recv,
    kv_send, kv_recv, kvf_send, kvf_recv,
    sa_send, sa_recv, saf_send, saf_recv, sb_send, sb_recv, sbf_send, sbf_recv,
):
    chip = lax.axis_index("req")
    core = lax.axis_index("kv")
    other = 1 - core
    sibling = (chip, other)
    z = lax.div(chip, SIDE * SIDE)
    plane = chip - z * (SIDE * SIDE)
    y = lax.div(plane, SIDE)
    x = plane - y * SIDE

    def wrap(at):
        return jnp.where(at >= SIDE, at - SIDE, at)

    across = [wrap(x + n) for n in range(SIDE)]

    def each_chip(do):
        def outer(a, za):
            def inner(b, yb):
                for n in range(SIDE):
                    there = wrap(za + n) * (SIDE * SIDE) + wrap(yb + n) * SIDE + across[n]
                    if n == 0:

                        @pl.when(a + b > 0)
                        def _():
                            do(a * (SIDE * SIDE) + b * SIDE, there)
                    else:
                        do(a * (SIDE * SIDE) + b * SIDE + n, there)
                return wrap(yb + 1)

            lax.fori_loop(0, SIDE, inner, y)
            return wrap(za + 1)

        lax.fori_loop(0, SIDE, outer, z)

    def local(src, dst, sem):
        return pltpu.make_async_copy(src, dst, sem)

    def remote(src, dst, send, recv, device):
        return pltpu.make_async_remote_copy(
            src_ref=src, dst_ref=dst, send_sem=send, recv_sem=recv, device_id=device, device_id_type=MESH
        )

    barrier = pltpu.get_barrier_semaphore()
    pl.semaphore_signal(barrier, inc=1, device_id=sibling, device_id_type=MESH)

    def greet(i, there):
        pl.semaphore_signal(barrier, inc=1, device_id=(there, core), device_id_type=MESH)

    each_chip(greet)

    ins = [
        local(rg, rgb, in_sem.at[0]),
        local(k, kvl.at[:, pl.ds(0, HALF)], in_sem.at[1]),
        local(v, kvl.at[:, pl.ds(HALF, HALF)], in_sem.at[2]),
        local(seg, segb.at[core], in_sem.at[3]),
        local(q.at[:, cols(core, HALF)], qb.at[rows_of(core), :], in_sem.at[4]),
        local(k.at[:, cols(core, KV_HALF)], kb.at[rows_of(core), :], in_sem.at[5]),
        local(v.at[:, cols(core, KV_HALF)], vb.at[rows_of(core), :], in_sem.at[6]),
        local(ag, ag_row, in_sem.at[7]),
        local(pg, pg_row, in_sem.at[8]),
        local(res, rb, in_sem.at[9]),
    ]
    for c in ins:
        c.start()

    def wrows(start, count):
        return wbuf.at[pl.ds(pl.multiple_of(start, CHUNK), count), :]

    def o_load(j):
        return local(ow.at[:, cols(j)], wrows(B_BASE + j * HALF, HALF), o_sem.at[j])

    for j in range(CHUNKS):
        o_load(j).start()

    def a_load(src, j, unit):
        return local(src.at[pl.ds(0, A_ROWS), cols(j)], wrows(unit * A_ROWS, A_ROWS), a_sem.at[unit])

    def b_start(unit):
        return B_BASE + lax.rem(unit, B_SLOTS) * B_ROWS

    def b_load(src, j, unit):
        return local(src.at[pl.ds(A_ROWS, B_ROWS), cols(j)], wrows(b_start(unit), B_ROWS), b_sem.at[unit])

    def d_start(j):
        return jnp.where(j < CHUNKS - 1, j * WIDTH, B_BASE + 6 * B_ROWS)

    def d_load(j):
        return local(dw.at[:, cols(j)], wrows(d_start(j), WIDTH), d_sem.at[j])

    for c in ins[:3]:
        c.wait()
    to = rgb[...]
    pick = lax.broadcasted_iota(jnp.int32, (ROWS, ROWS), 0) == lax.shift_right_logical(to, 7)
    pos = jnp.sum(
        jnp.where(pick, jnp.bitwise_and(to, 255).astype(F32), 0.0), axis=1, keepdims=True
    )
    pick = pick.astype(BF)
    pkv[:, :, KV_WIDTH:] = jnp.broadcast_to(pos, (ROWS, ROWS)).astype(BF).reshape(CHIPS, 2, ROWS)
    for j in range(KV_WIDTH // CHUNK):
        y_rows = jnp.dot(pick, kvl[:, cols(j)], preferred_element_type=F32).astype(BF)
        pkv[:, :, cols(j)] = y_rows.reshape(CHIPS, 2, CHUNK)

    pl.semaphore_wait(barrier, CHIPS)

    exchange = [
        remote(seg, segb.at[core], ex_send.at[0], ex_recv.at[0], sibling),
        remote(
            q.at[:, cols(other, HALF)], qb.at[rows_of(core), :], ex_send.at[1], ex_recv.at[1], sibling
        ),
        remote(
            k.at[:, cols(other, KV_HALF)], kb.at[rows_of(core), :], ex_send.at[2], ex_recv.at[2], sibling
        ),
        remote(
            v.at[:, cols(other, KV_HALF)], vb.at[rows_of(core), :], ex_send.at[3], ex_recv.at[3], sibling
        ),
    ]
    for c in exchange:
        c.start()

    def scatter(packets, landing, send, recv):
        here = local(packets.at[chip], landing.at[core, 0], recv.at[0])
        here.start()

        def one(i, there):
            group_of = i // PER_GROUP if isinstance(i, int) else lax.shift_right_logical(i, 3)
            remote(packets.at[there], landing.at[core, i], send, recv.at[group_of], (there, core)).start()

        each_chip(one)

    def scattered(packets, landing, send, recv):
        remote(
            packets.at[pl.ds(0, CHIPS - 1)], landing.at[core, pl.ds(0, CHIPS - 1)], send, recv.at[0], sibling
        ).wait_send()

    def group(i):
        return pl.ds(i * PER_GROUP, PER_GROUP)

    def forward(landing, i, send, recv):
        return remote(
            landing.at[core, group(i)], landing.at[core, group(i)], send.at[i], recv.at[i], sibling
        )

    def hand_on(landing, i, recv, send_f, recv_f):
        block = landing.at[core, group(i)]
        local(block, block, recv.at[i]).wait()
        forward(landing, i, send_f, recv_f).start()

    def arrive(landing, send_f, recv_f):
        def one(i, c):
            theirs = landing.at[other, group(i)]
            remote(theirs, theirs, send_f.at[i], recv_f.at[i], sibling).wait_recv()
            return c

        lax.fori_loop(0, GROUPS, one, 0)

    def hand_on_all(landing, recv, send_f, recv_f):
        def one(i, c):
            hand_on(landing, i, recv, send_f, recv_f)
            return c

        lax.fori_loop(0, GROUPS, one, 0)
        arrive(landing, send_f, recv_f)

    scatter(pkv, kvr, kv_send, kv_recv)

    for unit in range(UNITS):
        a_load((gw, uw)[unit % 2], unit // 2, unit).start()
    for unit in range(4, B_SLOTS):
        b_load((gw, uw)[unit % 2], unit // 2, unit).start()

    for c in ins[3:]:
        c.wait()
    for c in exchange:
        c.wait_recv()
    two = 2 * ROWS
    t_at = lax.broadcasted_iota(jnp.int32, (two, two), 0)
    s_at = lax.broadcasted_iota(jnp.int32, (two, two), 1)
    last = jnp.concatenate([segb[0], segb[1]], axis=1) - chip * two
    allowed = (s_at <= t_at) & (last >= t_at)
    for h in range(OWN_HEADS):
        own = pl.ds(h * HEAD, HEAD)
        key = pl.ds(h // 2 * HEAD, HEAD)
        raw = lax.dot_general(
            qb[:, own], kb[:, key], (((1,), (1,)), ((), ())), preferred_element_type=F32
        )
        scores = CAP * jnp.tanh(raw * (HEAD**-0.5 / CAP))
        probs = jnp.where(allowed, jnp.exp(scores), 0.0)
        totals = jnp.sum(probs, axis=-1, keepdims=True)
        mixed = jnp.dot(probs.astype(BF), vb[:, key], preferred_element_type=F32)
        att[:, own] = (mixed * (1.0 / totals)).astype(BF)

    def halves(landing, j, send, recv):
        return remote(
            part.at[rows_of(other), cols(j)], landing.at[:, cols(j)], send.at[j], recv.at[j], sibling
        )

    def project(j, c):
        o_load(j).wait()
        w = wrows(B_BASE + j * HALF, HALF)[...]
        part[:, cols(j)] = jnp.dot(att[...], w, preferred_element_type=F32).astype(BF)
        halves(prec, j, pr_send, pr_recv).start()
        return c

    lax.fori_loop(0, CHUNKS, project, 0)
    for unit in range(4):
        b_load((gw, uw)[unit % 2], unit // 2, unit).start()

    def sum_halves(j, squares):
        halves(prec, j, pr_send, pr_recv).wait_recv()
        both = part[rows_of(core), cols(j)].astype(F32) + prec[:, cols(j)].astype(F32)
        gacc[0:ROWS, cols(j)] = both
        return squares + lanes_sum(both * both)

    squares = lax.fori_loop(0, CHUNKS, sum_halves, jnp.zeros((ROWS, 128), F32))
    scale = lax.rsqrt(jnp.sum(squares, axis=-1, keepdims=True) * (1.0 / WIDTH) + EPS)

    def to_packets(packets, first):
        def one(j, c):
            at = cols(first + j)
            added = gacc[0:ROWS, at] * scale * ag_row[at].reshape(1, CHUNK)
            stream = (rb[:, at].astype(F32) + added).astype(BF)
            y_rows = jnp.dot(pick, stream, preferred_element_type=F32).astype(BF)
            packets[:, :, cols(j)] = y_rows.reshape(CHIPS, 2, CHUNK)
            return c

        return one

    lax.fori_loop(0, FIRST, to_packets(pka, 0), 0)
    scatter(pka, sta, sa_send, sa_recv)
    lax.fori_loop(0, SECOND, to_packets(pkb, FIRST), 0)

    hand_on_all(kvr, kv_recv, kvf_send, kvf_recv)
    at = kvr[:, :, :, KV_WIDTH:].reshape(two, 128).astype(F32)
    at = jnp.transpose(at)[0:1, :].astype(jnp.int32)
    place = (t_at == at).astype(BF)
    own_place = (t_at[0:ROWS, :] + core * ROWS == at).astype(BF)
    for j in range(KV_WIDTH // CHUNK):
        got = jnp.dot(
            own_place, kvr[:, :, :, cols(j)].reshape(two, CHUNK), preferred_element_type=F32
        ).astype(BF)
        kvo[2 * j] = got[:, 0:HEAD]
        kvo[2 * j + 1] = got[:, HEAD:]

    def put(landing, first):
        def one(j, squares):
            rows = landing[:, :, :, cols(j)].reshape(two, CHUNK)
            got = jnp.dot(place, rows, preferred_element_type=F32)
            at = cols(first + j)
            xb[:, at] = (got * pg_row[at].reshape(1, CHUNK)).astype(BF)
            own_rows[:, at] = jnp.dot(own_place, rows, preferred_element_type=F32).astype(BF)
            return squares + lanes_sum(got * got)

        return one

    scatter(pkb, stb, sb_send, sb_recv)
    hand_on_all(sta, sa_recv, saf_send, saf_recv)
    squares = lax.fori_loop(0, FIRST, put(sta, 0), jnp.zeros((two, 128), F32))

    def product(first, depth, start, i):
        w = wbuf[pl.ds(pl.multiple_of(start, CHUNK), depth), pl.ds(i * 256, 256)]
        return jnp.dot(xb[:, pl.ds(first, depth)], w, preferred_element_type=F32)

    def at256(j, i):
        return pl.ds(pl.multiple_of(j * CHUNK + i * 256, 256), 256)

    def begin(j, c):
        for m in range(2):
            a_load(gw, j, 2 * j + m).wait()
        for i in range(CHUNK // 256):
            gacc[:, at256(j, i)] = product(0, A_ROWS, 2 * j * A_ROWS, i)
            uacc[:, at256(j, i)] = product(0, A_ROWS, (2 * j + 1) * A_ROWS, i)

        @pl.when(j > 0)
        def _():
            d_load(j - 1).start()

        hand_on(stb, j, sb_recv, sbf_send, sbf_recv)
        return c

    lax.fori_loop(0, CHUNKS, begin, 0)
    hand_on(stb, CHUNKS, sb_recv, sbf_send, sbf_recv)
    arrive(stb, sbf_send, sbf_recv)
    squares = lax.fori_loop(0, SECOND, put(stb, FIRST), squares)
    scale = lax.rsqrt(jnp.sum(squares, axis=-1, keepdims=True) * (1.0 / WIDTH) + EPS)

    def hidden(j, c):
        for m in range(2):
            b_load(gw, j, 2 * j + m).wait()
        for i in range(CHUNK // 256):
            at = at256(j, i)
            u = (gacc[:, at] + product(A_ROWS, B_ROWS, b_start(2 * j), i)) * scale
            up = (uacc[:, at] + product(A_ROWS, B_ROWS, b_start(2 * j + 1), i)) * scale
            gelu = 0.5 * u * (1.0 + jnp.tanh(0.7978845608028654 * (u + 0.044715 * (u * u * u))))
            act[:, at] = (gelu * up).astype(BF)

        @pl.when(j < CHUNKS - B_SLOTS // 2)
        def _():
            b_load(gw, j + B_SLOTS // 2, 2 * j + B_SLOTS).start()
            b_load(uw, j + B_SLOTS // 2, 2 * j + 1 + B_SLOTS).start()

        @pl.when(j == CHUNKS - B_SLOTS // 2)
        def _():
            d_load(CHUNKS - 1).start()

        return c

    lax.fori_loop(0, CHUNKS, hidden, 0)

    def projected(j, c):
        halves(prec, j, pr_send, pr_recv).wait_send()
        return c

    lax.fori_loop(0, CHUNKS, projected, 0)

    def kept(j):
        return local(part.at[rows_of(core), cols(j)], mine.at[:, cols(j)], keep_sem.at[j])

    def down(j, c):
        d_load(j).wait()
        for i in range(CHUNK // 256):
            w = wbuf[pl.ds(pl.multiple_of(d_start(j), CHUNK), WIDTH), pl.ds(i * 256, 256)]
            part[:, at256(j, i)] = jnp.dot(act[...], w, preferred_element_type=F32).astype(BF)
        halves(theirs, j, dn_send, dn_recv).start()
        kept(j).start()
        return c

    lax.fori_loop(0, CHUNKS, down, 0)

    for c in exchange:
        c.wait_send()
    scattered(pkv, kvr, kv_send, kv_recv)
    scattered(pka, sta, sa_send, sa_recv)
    scattered(pkb, stb, sb_send, sb_recv)

    def sent(i, c):
        forward(kvr, i, kvf_send, kvf_recv).wait_send()
        forward(sta, i, saf_send, saf_recv).wait_send()
        forward(stb, i, sbf_send, sbf_recv).wait_send()
        return c

    lax.fori_loop(0, GROUPS, sent, 0)

    def down_sent(j, c):
        halves(theirs, j, dn_send, dn_recv).wait()
        kept(j).wait()
        return c

    lax.fori_loop(0, CHUNKS, down_sent, 0)


def last(mine, theirs, own_rows, kvo, og, lo, kc, vc, rows, og_row, kv_sem, og_sem, out_sem):
    def copy(src, dst, sem):
        return pltpu.make_async_copy(src, dst, sem)

    gain = copy(og, og_row, og_sem)
    gain.start()
    caches = [
        copy(kvo.at[pl.ds(0, 4)], kc, kv_sem.at[0]),
        copy(kvo.at[pl.ds(4, 4)], vc, kv_sem.at[1]),
    ]
    for c in caches:
        c.start()
    squares = jnp.zeros((ROWS, 128), F32)
    for j in range(CHUNKS):
        both = mine[:, cols(j)].astype(F32) + theirs[:, cols(j)].astype(F32)
        squares = squares + lanes_sum(both * both)
    scale = lax.rsqrt(jnp.sum(squares, axis=-1, keepdims=True) * (1.0 / WIDTH) + EPS)
    gain.wait()

    def store(j):
        return copy(rows.at[:, cols(j)], lo.at[:, cols(j)], out_sem.at[j])

    for j in range(CHUNKS):
        both = mine[:, cols(j)].astype(F32) + theirs[:, cols(j)].astype(F32)
        row = og_row[cols(j)].reshape(1, CHUNK)
        rows[:, cols(j)] = (own_rows[:, cols(j)].astype(F32) + both * scale * row).astype(BF)
        store(j).start()
    for j in range(CHUNKS):
        store(j).wait()
    for c in caches:
        c.wait()


def per_device(
    queries,
    keys,
    values,
    residual,
    segment_ids,
    regroup,
    out_weight,
    attn_gain,
    pre_gain,
    gate_weight,
    up_weight,
    down_weight,
    post_gain,
):
    dma = pltpu.SemaphoreType.DMA
    vmem = pltpu.VMEM
    mine, theirs, own_rows, kvo = pl.pallas_call(
        kernel,
        out_shape=(
            vmem((ROWS, WIDTH), BF),
            vmem((ROWS, WIDTH), BF),
            vmem((ROWS, WIDTH), BF),
            vmem((8, ROWS, HEAD), BF),
        ),
        in_specs=[pl.BlockSpec(memory_space=pl.ANY)] * 12,
        out_specs=(pl.BlockSpec(memory_space=vmem),) * 4,
        scratch_shapes=[
            vmem((B_BASE + B_SLOTS * B_ROWS, CHUNK), BF),
            vmem((2 * ROWS, HALF), BF),
            vmem((2 * ROWS, KV_HALF), BF),
            vmem((2 * ROWS, KV_HALF), BF),
            vmem((2, 1, ROWS), jnp.int32),
            vmem((ROWS, KV_WIDTH), BF),
            vmem((1, ROWS), jnp.int32),
            vmem((WIDTH,), F32),
            vmem((WIDTH,), F32),
            vmem((ROWS, WIDTH), BF),
            vmem((2 * ROWS, HALF), BF),
            vmem((2 * ROWS, WIDTH), BF),
            vmem((ROWS, WIDTH), BF),
            vmem((CHIPS, 2, KV_WIDTH + 128), BF),
            vmem((2, CHIPS, 2, KV_WIDTH + 128), BF),
            vmem((CHIPS, 2, A_ROWS), BF),
            vmem((CHIPS, 2, B_ROWS), BF),
            vmem((2, CHIPS, 2, A_ROWS), BF),
            vmem((2, CHIPS, 2, B_ROWS), BF),
            vmem((2 * ROWS, WIDTH), BF),
            vmem((2 * ROWS, WIDTH), BF),
            vmem((2 * ROWS, WIDTH), F32),
            vmem((2 * ROWS, WIDTH), F32),
            dma((10,)),
            dma((CHUNKS,)),
            dma((UNITS,)),
            dma((UNITS,)),
            dma((CHUNKS,)),
            dma((CHUNKS,)),
            dma((4,)),
            dma((4,)),
            dma((CHUNKS,)),
            dma((CHUNKS,)),
            dma((CHUNKS,)),
            dma((CHUNKS,)),
            *[dma, dma((GROUPS,)), dma((GROUPS,)), dma((GROUPS,))] * 3,
        ],
        compiler_params=pltpu.CompilerParams(
            collective_id=0, has_side_effects=True, vmem_limit_bytes=60 * 1024 * 1024
        ),
        name="layer",
    )(
        queries,
        keys,
        values,
        residual,
        segment_ids.reshape(1, ROWS),
        regroup.reshape(1, ROWS),
        out_weight,
        attn_gain,
        pre_gain,
        gate_weight,
        up_weight,
        down_weight,
    )
    return pl.pallas_call(
        last,
        out_shape=(
            jax.ShapeDtypeStruct((ROWS, WIDTH), BF),
            jax.ShapeDtypeStruct((4, ROWS, HEAD), BF),
            jax.ShapeDtypeStruct((4, ROWS, HEAD), BF),
        ),
        in_specs=[pl.BlockSpec(memory_space=vmem)] * 4 + [pl.BlockSpec(memory_space=pl.ANY)],
        out_specs=(pl.BlockSpec(memory_space=pl.ANY),) * 3,
        scratch_shapes=[
            vmem((ROWS, WIDTH), BF),
            vmem((WIDTH,), F32),
            dma((2,)),
            dma,
            dma((CHUNKS,)),
        ],
        compiler_params=pltpu.CompilerParams(vmem_limit_bytes=60 * 1024 * 1024),
        name="last",
    )(*(pltpu.with_memory_space_constraint(r, vmem) for r in (mine, theirs, own_rows, kvo)), post_gain)


def solution(mesh):
    rows = P(("req", "kv"), None)
    flat = P(("req", "kv"))
    return jax.shard_map(
        per_device,
        mesh=mesh,
        in_specs=(
            rows, rows, rows, rows, flat, flat, P("kv", None), P(), P(),
            P(None, "kv"), P(None, "kv"), P("kv", None), P(),
        ),
        out_specs=(rows, P(None, ("req", "kv"), None), P(None, ("req", "kv"), None)),
        check_vma=False,
    )
```

```python
import jax
import jax.numpy as jnp
from jax import lax
from jax.experimental import pallas as pl
from jax.experimental.pallas import tpu as pltpu
from jax.sharding import PartitionSpec as P

MESH = pl.DeviceIdType.MESH
CHIPS = 64
SIDE = 4
ROWS = 128
WIDTH = 3584
HEAD = 256
OWN_HEADS = 4
HALF = 1024
KV_HALF = 512
KV_WIDTH = 2048
CHUNK = 512
CHUNKS = WIDTH // CHUNK
FIRST = 3
SECOND = CHUNKS - FIRST
A_ROWS = FIRST * CHUNK
B_ROWS = SECOND * CHUNK
UNITS = 2 * CHUNKS
B_SLOTS = 8
B_BASE = UNITS * A_ROWS
GROUPS = 8
PER_GROUP = CHIPS // GROUPS
CAP = 50.0
EPS = 1e-06
BF = jnp.bfloat16
F32 = jnp.float32


def cols(j, width=CHUNK):
    if isinstance(j, int):
        return pl.ds(j * width, width)
    return pl.ds(pl.multiple_of(j * width, width), width)


def rows_of(core):
    return pl.ds(pl.multiple_of(core * ROWS, ROWS), ROWS)


def lanes_sum(value):
    total = value[:, 0:128]
    for i in range(1, CHUNK // 128):
        total = total + value[:, i * 128 : (i + 1) * 128]
    return total


def kernel(
    q, k, v, res, seg, rg, ow, ag, pg, gw, uw, dw,
    mine, theirs, own_rows, kvo,
    wbuf, qb, kb, vb, segb, kvl, rgb, ag_row, pg_row, rb, att, part, prec, pkv, kvr, pka, pkb, sta, stb,
    xb, act, gacc, uacc,
    in_sem, o_sem, a_sem, b_sem, d_sem, keep_sem, ex_send, ex_recv, pr_send, pr_recv, dn_send, dn_recv,
    kv_send, kv_recv, kvf_send, kvf_recv,
    sa_send, sa_recv, saf_send, saf_recv, sb_send, sb_recv, sbf_send, sbf_recv,
):
    chip = lax.axis_index("req")
    core = lax.axis_index("kv")
    other = 1 - core
    sibling = (chip, other)
    z = lax.div(chip, SIDE * SIDE)
    plane = chip - z * (SIDE * SIDE)
    y = lax.div(plane, SIDE)
    x = plane - y * SIDE

    def wrap(at):
        return jnp.where(at >= SIDE, at - SIDE, at)

    across = [wrap(x + n) for n in range(SIDE)]

    def each_chip(do):
        def outer(a, za):
            def inner(b, yb):
                for n in range(SIDE):
                    there = wrap(za + n) * (SIDE * SIDE) + wrap(yb + n) * SIDE + across[n]
                    if n == 0:

                        @pl.when(a + b > 0)
                        def _():
                            do(a * (SIDE * SIDE) + b * SIDE, there)
                    else:
                        do(a * (SIDE * SIDE) + b * SIDE + n, there)
                return wrap(yb + 1)

            lax.fori_loop(0, SIDE, inner, y)
            return wrap(za + 1)

        lax.fori_loop(0, SIDE, outer, z)

    def local(src, dst, sem):
        return pltpu.make_async_copy(src, dst, sem)

    def remote(src, dst, send, recv, device):
        return pltpu.make_async_remote_copy(
            src_ref=src, dst_ref=dst, send_sem=send, recv_sem=recv, device_id=device, device_id_type=MESH
        )

    barrier = pltpu.get_barrier_semaphore()
    pl.semaphore_signal(barrier, inc=1, device_id=sibling, device_id_type=MESH)

    def greet(i, there):
        pl.semaphore_signal(barrier, inc=1, device_id=(there, core), device_id_type=MESH)

    each_chip(greet)

    ins = [
        local(rg, rgb, in_sem.at[0]),
        local(k, kvl.at[:, pl.ds(0, HALF)], in_sem.at[1]),
        local(v, kvl.at[:, pl.ds(HALF, HALF)], in_sem.at[2]),
        local(seg, segb.at[core], in_sem.at[3]),
        local(q.at[:, cols(core, HALF)], qb.at[rows_of(core), :], in_sem.at[4]),
        local(k.at[:, cols(core, KV_HALF)], kb.at[rows_of(core), :], in_sem.at[5]),
        local(v.at[:, cols(core, KV_HALF)], vb.at[rows_of(core), :], in_sem.at[6]),
        local(ag, ag_row, in_sem.at[7]),
        local(pg, pg_row, in_sem.at[8]),
        local(res, rb, in_sem.at[9]),
    ]
    for c in ins:
        c.start()

    def wrows(start, count):
        return wbuf.at[pl.ds(pl.multiple_of(start, CHUNK), count), :]

    def o_load(j):
        return local(ow.at[:, cols(j)], wrows(B_BASE + j * HALF, HALF), o_sem.at[j])

    for j in range(CHUNKS):
        o_load(j).start()

    def a_load(src, j, unit):
        return local(src.at[pl.ds(0, A_ROWS), cols(j)], wrows(unit * A_ROWS, A_ROWS), a_sem.at[unit])

    def b_start(unit):
        return B_BASE + lax.rem(unit, B_SLOTS) * B_ROWS

    def b_load(src, j, unit):
        return local(src.at[pl.ds(A_ROWS, B_ROWS), cols(j)], wrows(b_start(unit), B_ROWS), b_sem.at[unit])

    def d_start(j):
        return jnp.where(j < CHUNKS - 1, j * WIDTH, B_BASE + 6 * B_ROWS)

    def d_load(j):
        return local(dw.at[:, cols(j)], wrows(d_start(j), WIDTH), d_sem.at[j])

    for c in ins[:3]:
        c.wait()
    to = rgb[...]
    pick = lax.broadcasted_iota(jnp.int32, (ROWS, ROWS), 0) == lax.shift_right_logical(to, 7)
    pos = jnp.sum(
        jnp.where(pick, jnp.bitwise_and(to, 255).astype(F32), 0.0), axis=1, keepdims=True
    )
    pick = pick.astype(BF)
    pkv[:, :, KV_WIDTH:] = jnp.broadcast_to(pos, (ROWS, ROWS)).astype(BF).reshape(CHIPS, 2, ROWS)
    for j in range(KV_WIDTH // CHUNK):
        y_rows = jnp.dot(pick, kvl[:, cols(j)], preferred_element_type=F32).astype(BF)
        pkv[:, :, cols(j)] = y_rows.reshape(CHIPS, 2, CHUNK)

    pl.semaphore_wait(barrier, CHIPS)

    exchange = [
        remote(seg, segb.at[core], ex_send.at[0], ex_recv.at[0], sibling),
        remote(
            q.at[:, cols(other, HALF)], qb.at[rows_of(core), :], ex_send.at[1], ex_recv.at[1], sibling
        ),
        remote(
            k.at[:, cols(other, KV_HALF)], kb.at[rows_of(core), :], ex_send.at[2], ex_recv.at[2], sibling
        ),
        remote(
            v.at[:, cols(other, KV_HALF)], vb.at[rows_of(core), :], ex_send.at[3], ex_recv.at[3], sibling
        ),
    ]
    for c in exchange:
        c.start()

    def scatter(packets, landing, send, recv):
        here = local(packets.at[chip], landing.at[core, 0], recv.at[0])
        here.start()

        def one(i, there):
            group_of = i // PER_GROUP if isinstance(i, int) else lax.shift_right_logical(i, 3)
            remote(packets.at[there], landing.at[core, i], send, recv.at[group_of], (there, core)).start()

        each_chip(one)

    def scattered(packets, landing, send, recv):
        remote(
            packets.at[pl.ds(0, CHIPS - 1)], landing.at[core, pl.ds(0, CHIPS - 1)], send, recv.at[0], sibling
        ).wait_send()

    def group(i):
        return pl.ds(i * PER_GROUP, PER_GROUP)

    def forward(landing, i, send, recv):
        return remote(
            landing.at[core, group(i)], landing.at[core, group(i)], send.at[i], recv.at[i], sibling
        )

    def hand_on(landing, i, recv, send_f, recv_f):
        block = landing.at[core, group(i)]
        local(block, block, recv.at[i]).wait()
        forward(landing, i, send_f, recv_f).start()

    def arrive(landing, send_f, recv_f):
        def one(i, c):
            theirs = landing.at[other, group(i)]
            remote(theirs, theirs, send_f.at[i], recv_f.at[i], sibling).wait_recv()
            return c

        lax.fori_loop(0, GROUPS, one, 0)

    def hand_on_all(landing, recv, send_f, recv_f):
        def one(i, c):
            hand_on(landing, i, recv, send_f, recv_f)
            return c

        lax.fori_loop(0, GROUPS, one, 0)
        arrive(landing, send_f, recv_f)

    scatter(pkv, kvr, kv_send, kv_recv)

    for unit in range(UNITS):
        a_load((gw, uw)[unit % 2], unit // 2, unit).start()
    for unit in range(4, B_SLOTS):
        b_load((gw, uw)[unit % 2], unit // 2, unit).start()

    for c in ins[3:7]:
        c.wait()
    for c in exchange[:3]:
        c.wait_recv()
    two = 2 * ROWS
    t_at = lax.broadcasted_iota(jnp.int32, (two, two), 0)
    s_at = lax.broadcasted_iota(jnp.int32, (two, two), 1)
    last = jnp.concatenate([segb[0], segb[1]], axis=1) - chip * two
    allowed = (s_at <= t_at) & (last >= t_at)
    for h in range(OWN_HEADS):
        own = pl.ds(h * HEAD, HEAD)
        key = pl.ds(h // 2 * HEAD, HEAD)
        raw = lax.dot_general(
            qb[:, own], kb[:, key], (((1,), (1,)), ((), ())), preferred_element_type=F32
        )
        scores = CAP * jnp.tanh(raw * (HEAD**-0.5 / CAP))
        probs = jnp.where(allowed, jnp.exp(scores), 0.0)
        totals = jnp.sum(probs, axis=-1, keepdims=True)
        if h == 0:
            exchange[3].wait_recv()
        mixed = jnp.dot(probs.astype(BF), vb[:, key], preferred_element_type=F32)
        att[:, own] = (mixed * (1.0 / totals)).astype(BF)

    def halves(landing, j, send, recv):
        return remote(
            part.at[rows_of(other), cols(j)], landing.at[:, cols(j)], send.at[j], recv.at[j], sibling
        )

    def project(j, c):
        o_load(j).wait()
        w = wrows(B_BASE + j * HALF, HALF)[...]
        part[:, cols(j)] = jnp.dot(att[...], w, preferred_element_type=F32).astype(BF)
        halves(prec, j, pr_send, pr_recv).start()
        return c

    lax.fori_loop(0, CHUNKS, project, 0)
    for unit in range(4):
        b_load((gw, uw)[unit % 2], unit // 2, unit).start()

    def sum_halves(j, squares):
        halves(prec, j, pr_send, pr_recv).wait_recv()
        both = part[rows_of(core), cols(j)].astype(F32) + prec[:, cols(j)].astype(F32)
        gacc[0:ROWS, cols(j)] = both
        return squares + lanes_sum(both * both)

    squares = lax.fori_loop(0, CHUNKS, sum_halves, jnp.zeros((ROWS, 128), F32))
    scale = lax.rsqrt(jnp.sum(squares, axis=-1, keepdims=True) * (1.0 / WIDTH) + EPS)

    def to_packets(packets, first):
        def one(j, c):
            at = cols(first + j)
            added = gacc[0:ROWS, at] * scale * ag_row[at].reshape(1, CHUNK)
            stream = (rb[:, at].astype(F32) + added).astype(BF)
            y_rows = jnp.dot(pick, stream, preferred_element_type=F32).astype(BF)
            packets[:, :, cols(j)] = y_rows.reshape(CHIPS, 2, CHUNK)
            return c

        return one

    for c in ins[7:]:
        c.wait()
    lax.fori_loop(0, FIRST, to_packets(pka, 0), 0)
    scatter(pka, sta, sa_send, sa_recv)
    lax.fori_loop(0, SECOND, to_packets(pkb, FIRST), 0)

    hand_on_all(kvr, kv_recv, kvf_send, kvf_recv)
    at = kvr[:, :, :, KV_WIDTH:].reshape(two, 128).astype(F32)
    at = jnp.transpose(at)[0:1, :].astype(jnp.int32)
    place = (t_at == at).astype(BF)
    own_place = (t_at[0:ROWS, :] + core * ROWS == at).astype(BF)
    for j in range(KV_WIDTH // CHUNK):
        got = jnp.dot(
            own_place, kvr[:, :, :, cols(j)].reshape(two, CHUNK), preferred_element_type=F32
        ).astype(BF)
        kvo[2 * j] = got[:, 0:HEAD]
        kvo[2 * j + 1] = got[:, HEAD:]

    def put(landing, first):
        def one(j, squares):
            rows = landing[:, :, :, cols(j)].reshape(two, CHUNK)
            got = jnp.dot(place, rows, preferred_element_type=F32)
            at = cols(first + j)
            xb[:, at] = (got * pg_row[at].reshape(1, CHUNK)).astype(BF)
            own_rows[:, at] = jnp.dot(own_place, rows, preferred_element_type=F32).astype(BF)
            return squares + lanes_sum(got * got)

        return one

    scatter(pkb, stb, sb_send, sb_recv)
    hand_on_all(sta, sa_recv, saf_send, saf_recv)
    squares = lax.fori_loop(0, FIRST, put(sta, 0), jnp.zeros((two, 128), F32))

    def product(first, depth, start, i):
        w = wbuf[pl.ds(pl.multiple_of(start, CHUNK), depth), pl.ds(i * 256, 256)]
        return jnp.dot(xb[:, pl.ds(first, depth)], w, preferred_element_type=F32)

    def at256(j, i):
        return pl.ds(pl.multiple_of(j * CHUNK + i * 256, 256), 256)

    def begin(j, c):
        for m in range(2):
            a_load(gw, j, 2 * j + m).wait()
        for i in range(CHUNK // 256):
            gacc[:, at256(j, i)] = product(0, A_ROWS, 2 * j * A_ROWS, i)
            uacc[:, at256(j, i)] = product(0, A_ROWS, (2 * j + 1) * A_ROWS, i)

        @pl.when(j > 0)
        def _():
            d_load(j - 1).start()

        hand_on(stb, j, sb_recv, sbf_send, sbf_recv)
        return c

    lax.fori_loop(0, CHUNKS, begin, 0)
    hand_on(stb, CHUNKS, sb_recv, sbf_send, sbf_recv)
    arrive(stb, sbf_send, sbf_recv)
    squares = lax.fori_loop(0, SECOND, put(stb, FIRST), squares)
    scale = lax.rsqrt(jnp.sum(squares, axis=-1, keepdims=True) * (1.0 / WIDTH) + EPS)

    def hidden(j, c):
        for m in range(2):
            b_load(gw, j, 2 * j + m).wait()
        for i in range(CHUNK // 256):
            at = at256(j, i)
            u = (gacc[:, at] + product(A_ROWS, B_ROWS, b_start(2 * j), i)) * scale
            up = (uacc[:, at] + product(A_ROWS, B_ROWS, b_start(2 * j + 1), i)) * scale
            gelu = 0.5 * u * (1.0 + jnp.tanh(0.7978845608028654 * (u + 0.044715 * (u * u * u))))
            act[:, at] = (gelu * up).astype(BF)

        @pl.when(j < CHUNKS - B_SLOTS // 2)
        def _():
            b_load(gw, j + B_SLOTS // 2, 2 * j + B_SLOTS).start()
            b_load(uw, j + B_SLOTS // 2, 2 * j + 1 + B_SLOTS).start()

        @pl.when(j == CHUNKS - B_SLOTS // 2)
        def _():
            d_load(CHUNKS - 1).start()

        return c

    lax.fori_loop(0, CHUNKS, hidden, 0)

    def projected(j, c):
        halves(prec, j, pr_send, pr_recv).wait_send()
        return c

    lax.fori_loop(0, CHUNKS, projected, 0)

    def kept(j):
        return local(part.at[rows_of(core), cols(j)], mine.at[:, cols(j)], keep_sem.at[j])

    def down(j, c):
        d_load(j).wait()
        for i in range(CHUNK // 256):
            w = wbuf[pl.ds(pl.multiple_of(d_start(j), CHUNK), WIDTH), pl.ds(i * 256, 256)]
            part[:, at256(j, i)] = jnp.dot(act[...], w, preferred_element_type=F32).astype(BF)
        halves(theirs, j, dn_send, dn_recv).start()
        kept(j).start()
        return c

    lax.fori_loop(0, CHUNKS - 1, down, 0)
    end = CHUNKS - 1
    d_load(end).wait()

    def end_product(rows, i):
        w = wbuf[pl.ds(B_BASE + 6 * B_ROWS, WIDTH), pl.ds(i * 256, 256)]
        return jnp.dot(act[rows, :], w, preferred_element_type=F32).astype(BF)

    for i in range(CHUNK // 256):
        part[rows_of(other), pl.ds(end * CHUNK + i * 256, 256)] = end_product(rows_of(other), i)
    halves(theirs, end, dn_send, dn_recv).start()
    for i in range(CHUNK // 256):
        mine[:, pl.ds(end * CHUNK + i * 256, 256)] = end_product(rows_of(core), i)

    for c in exchange:
        c.wait_send()
    scattered(pkv, kvr, kv_send, kv_recv)
    scattered(pka, sta, sa_send, sa_recv)
    scattered(pkb, stb, sb_send, sb_recv)

    def sent(i, c):
        forward(kvr, i, kvf_send, kvf_recv).wait_send()
        forward(sta, i, saf_send, saf_recv).wait_send()
        forward(stb, i, sbf_send, sbf_recv).wait_send()
        return c

    lax.fori_loop(0, GROUPS, sent, 0)

    def down_sent(j, c):
        halves(theirs, j, dn_send, dn_recv).wait()
        return c

    lax.fori_loop(0, CHUNKS, down_sent, 0)

    def kept_all(j, c):
        kept(j).wait()
        return c

    lax.fori_loop(0, CHUNKS - 1, kept_all, 0)


def last(mine, theirs, own_rows, kvo, og, lo, kc, vc, rows, og_row, kv_sem, og_sem, out_sem):
    def copy(src, dst, sem):
        return pltpu.make_async_copy(src, dst, sem)

    gain = copy(og, og_row, og_sem)
    gain.start()
    caches = [
        copy(kvo.at[pl.ds(0, 4)], kc, kv_sem.at[0]),
        copy(kvo.at[pl.ds(4, 4)], vc, kv_sem.at[1]),
    ]
    for c in caches:
        c.start()
    squares = jnp.zeros((ROWS, 128), F32)
    for j in range(CHUNKS):
        both = mine[:, cols(j)].astype(F32) + theirs[:, cols(j)].astype(F32)
        squares = squares + lanes_sum(both * both)
    scale = lax.rsqrt(jnp.sum(squares, axis=-1, keepdims=True) * (1.0 / WIDTH) + EPS)
    gain.wait()

    def store(j):
        return copy(rows.at[:, cols(j)], lo.at[:, cols(j)], out_sem.at[j])

    for j in range(CHUNKS):
        both = mine[:, cols(j)].astype(F32) + theirs[:, cols(j)].astype(F32)
        row = og_row[cols(j)].reshape(1, CHUNK)
        rows[:, cols(j)] = (own_rows[:, cols(j)].astype(F32) + both * scale * row).astype(BF)
        store(j).start()
    for j in range(CHUNKS):
        store(j).wait()
    for c in caches:
        c.wait()


def per_device(
    queries,
    keys,
    values,
    residual,
    segment_ids,
    regroup,
    out_weight,
    attn_gain,
    pre_gain,
    gate_weight,
    up_weight,
    down_weight,
    post_gain,
):
    dma = pltpu.SemaphoreType.DMA
    vmem = pltpu.VMEM
    mine, theirs, own_rows, kvo = pl.pallas_call(
        kernel,
        out_shape=(
            vmem((ROWS, WIDTH), BF),
            vmem((ROWS, WIDTH), BF),
            vmem((ROWS, WIDTH), BF),
            vmem((8, ROWS, HEAD), BF),
        ),
        in_specs=[pl.BlockSpec(memory_space=pl.ANY)] * 12,
        out_specs=(pl.BlockSpec(memory_space=vmem),) * 4,
        scratch_shapes=[
            vmem((B_BASE + B_SLOTS * B_ROWS, CHUNK), BF),
            vmem((2 * ROWS, HALF), BF),
            vmem((2 * ROWS, KV_HALF), BF),
            vmem((2 * ROWS, KV_HALF), BF),
            vmem((2, 1, ROWS), jnp.int32),
            vmem((ROWS, KV_WIDTH), BF),
            vmem((1, ROWS), jnp.int32),
            vmem((WIDTH,), F32),
            vmem((WIDTH,), F32),
            vmem((ROWS, WIDTH), BF),
            vmem((2 * ROWS, HALF), BF),
            vmem((2 * ROWS, WIDTH), BF),
            vmem((ROWS, WIDTH), BF),
            vmem((CHIPS, 2, KV_WIDTH + 128), BF),
            vmem((2, CHIPS, 2, KV_WIDTH + 128), BF),
            vmem((CHIPS, 2, A_ROWS), BF),
            vmem((CHIPS, 2, B_ROWS), BF),
            vmem((2, CHIPS, 2, A_ROWS), BF),
            vmem((2, CHIPS, 2, B_ROWS), BF),
            vmem((2 * ROWS, WIDTH), BF),
            vmem((2 * ROWS, WIDTH), BF),
            vmem((2 * ROWS, WIDTH), F32),
            vmem((2 * ROWS, WIDTH), F32),
            dma((10,)),
            dma((CHUNKS,)),
            dma((UNITS,)),
            dma((UNITS,)),
            dma((CHUNKS,)),
            dma((CHUNKS,)),
            dma((4,)),
            dma((4,)),
            dma((CHUNKS,)),
            dma((CHUNKS,)),
            dma((CHUNKS,)),
            dma((CHUNKS,)),
            *[dma, dma((GROUPS,)), dma((GROUPS,)), dma((GROUPS,))] * 3,
        ],
        compiler_params=pltpu.CompilerParams(
            collective_id=0, has_side_effects=True, vmem_limit_bytes=60 * 1024 * 1024
        ),
        name="layer",
    )(
        queries,
        keys,
        values,
        residual,
        segment_ids.reshape(1, ROWS),
        regroup.reshape(1, ROWS),
        out_weight,
        attn_gain,
        pre_gain,
        gate_weight,
        up_weight,
        down_weight,
    )
    return pl.pallas_call(
        last,
        out_shape=(
            jax.ShapeDtypeStruct((ROWS, WIDTH), BF),
            jax.ShapeDtypeStruct((4, ROWS, HEAD), BF),
            jax.ShapeDtypeStruct((4, ROWS, HEAD), BF),
        ),
        in_specs=[pl.BlockSpec(memory_space=vmem)] * 4 + [pl.BlockSpec(memory_space=pl.ANY)],
        out_specs=(pl.BlockSpec(memory_space=pl.ANY),) * 3,
        scratch_shapes=[
            vmem((ROWS, WIDTH), BF),
            vmem((WIDTH,), F32),
            dma((2,)),
            dma,
            dma((CHUNKS,)),
        ],
        compiler_params=pltpu.CompilerParams(vmem_limit_bytes=60 * 1024 * 1024),
        name="last",
    )(*(pltpu.with_memory_space_constraint(r, vmem) for r in (mine, theirs, own_rows, kvo)), post_gain)


def solution(mesh):
    rows = P(("req", "kv"), None)
    flat = P(("req", "kv"))
    return jax.shard_map(
        per_device,
        mesh=mesh,
        in_specs=(
            rows, rows, rows, rows, flat, flat, P("kv", None), P(), P(),
            P(None, "kv"), P(None, "kv"), P("kv", None), P(),
        ),
        out_specs=(rows, P(None, ("req", "kv"), None), P(None, ("req", "kv"), None)),
        check_vma=False,
    )
```

```python
import jax
import jax.numpy as jnp
from jax import lax
from jax.experimental import pallas as pl
from jax.experimental.pallas import tpu as pltpu
from jax.sharding import PartitionSpec as P

MESH = pl.DeviceIdType.MESH
CHIPS = 64
SIDE = 4
ROWS = 128
WIDTH = 3584
HEAD = 256
OWN_HEADS = 4
HALF = 1024
KV_HALF = 512
KV_WIDTH = 2048
CHUNK = 512
CHUNKS = WIDTH // CHUNK
FIRST = 3
SECOND = CHUNKS - FIRST
A_ROWS = FIRST * CHUNK
B_ROWS = SECOND * CHUNK
UNITS = 2 * CHUNKS
B_SLOTS = 8
B_BASE = UNITS * A_ROWS
GROUPS = 8
PER_GROUP = CHIPS // GROUPS
CAP = 50.0
EPS = 1e-06
BF = jnp.bfloat16
F32 = jnp.float32


def cols(j, width=CHUNK):
    if isinstance(j, int):
        return pl.ds(j * width, width)
    return pl.ds(pl.multiple_of(j * width, width), width)


def rows_of(core):
    return pl.ds(pl.multiple_of(core * ROWS, ROWS), ROWS)


def lanes_sum(value):
    total = value[:, 0:128]
    for i in range(1, CHUNK // 128):
        total = total + value[:, i * 128 : (i + 1) * 128]
    return total


def kernel(
    q, k, v, res, seg, rg, ow, ag, pg, gw, uw, dw,
    mine, theirs, own_rows, kvo,
    wbuf, qb, kb, vb, segb, kvl, rgb, ag_row, pg_row, rb, att, part, prec, pkv, kvr, pka, pkb, sta, stb,
    xb, act, gacc, uacc,
    in_sem, o_sem, a_sem, b_sem, d_sem, keep_sem, ex_send, ex_recv, pr_send, pr_recv, dn_send, dn_recv,
    kv_send, kv_recv, kvf_send, kvf_recv,
    sa_send, sa_recv, saf_send, saf_recv, sb_send, sb_recv, sbf_send, sbf_recv,
):
    chip = lax.axis_index("req")
    core = lax.axis_index("kv")
    other = 1 - core
    sibling = (chip, other)
    z = lax.div(chip, SIDE * SIDE)
    plane = chip - z * (SIDE * SIDE)
    y = lax.div(plane, SIDE)
    x = plane - y * SIDE

    def wrap(at):
        return jnp.where(at >= SIDE, at - SIDE, at)

    across = [wrap(x + n) for n in range(SIDE)]

    def each_chip(do):
        def outer(a, za):
            def inner(b, yb):
                for n in range(SIDE):
                    there = wrap(za + n) * (SIDE * SIDE) + wrap(yb + n) * SIDE + across[n]
                    if n == 0:

                        @pl.when(a + b > 0)
                        def _():
                            do(a * (SIDE * SIDE) + b * SIDE, there)
                    else:
                        do(a * (SIDE * SIDE) + b * SIDE + n, there)
                return wrap(yb + 1)

            lax.fori_loop(0, SIDE, inner, y)
            return wrap(za + 1)

        lax.fori_loop(0, SIDE, outer, z)

    def local(src, dst, sem):
        return pltpu.make_async_copy(src, dst, sem)

    def remote(src, dst, send, recv, device):
        return pltpu.make_async_remote_copy(
            src_ref=src, dst_ref=dst, send_sem=send, recv_sem=recv, device_id=device, device_id_type=MESH
        )

    barrier = pltpu.get_barrier_semaphore()
    pl.semaphore_signal(barrier, inc=1, device_id=sibling, device_id_type=MESH)

    def greet(i, there):
        pl.semaphore_signal(barrier, inc=1, device_id=(there, core), device_id_type=MESH)

    each_chip(greet)

    ins = [
        local(rg, rgb, in_sem.at[0]),
        local(k, kvl.at[:, pl.ds(0, HALF)], in_sem.at[1]),
        local(v, kvl.at[:, pl.ds(HALF, HALF)], in_sem.at[2]),
        local(seg, segb.at[core], in_sem.at[3]),
        local(q.at[:, cols(core, HALF)], qb.at[rows_of(core), :], in_sem.at[4]),
        local(k.at[:, cols(core, KV_HALF)], kb.at[rows_of(core), :], in_sem.at[5]),
        local(v.at[:, cols(core, KV_HALF)], vb.at[rows_of(core), :], in_sem.at[6]),
        local(ag, ag_row, in_sem.at[7]),
        local(pg, pg_row, in_sem.at[8]),
        local(res, rb, in_sem.at[9]),
    ]
    for c in ins:
        c.start()

    def wrows(start, count):
        return wbuf.at[pl.ds(pl.multiple_of(start, CHUNK), count), :]

    def o_load(j):
        return local(ow.at[:, cols(j)], wrows(B_BASE + j * HALF, HALF), o_sem.at[j])

    for j in range(CHUNKS):
        o_load(j).start()

    def a_load(src, j, unit):
        return local(src.at[pl.ds(0, A_ROWS), cols(j)], wrows(unit * A_ROWS, A_ROWS), a_sem.at[unit])

    def b_start(unit):
        return B_BASE + lax.rem(unit, B_SLOTS) * B_ROWS

    def b_load(src, j, unit):
        return local(src.at[pl.ds(A_ROWS, B_ROWS), cols(j)], wrows(b_start(unit), B_ROWS), b_sem.at[unit])

    def d_start(j):
        return jnp.where(j < CHUNKS - 1, j * WIDTH, B_BASE + 6 * B_ROWS)

    def d_load(j):
        return local(dw.at[:, cols(j)], wrows(d_start(j), WIDTH), d_sem.at[j])

    for c in ins[:3]:
        c.wait()
    to = rgb[...]
    pick = lax.broadcasted_iota(jnp.int32, (ROWS, ROWS), 0) == lax.shift_right_logical(to, 7)
    pos = jnp.sum(
        jnp.where(pick, jnp.bitwise_and(to, 255).astype(F32), 0.0), axis=1, keepdims=True
    )
    pick = pick.astype(BF)
    pkv[:, :, KV_WIDTH:] = jnp.broadcast_to(pos, (ROWS, ROWS)).astype(BF).reshape(CHIPS, 2, ROWS)
    for j in range(KV_WIDTH // CHUNK):
        y_rows = jnp.dot(pick, kvl[:, cols(j)], preferred_element_type=F32).astype(BF)
        pkv[:, :, cols(j)] = y_rows.reshape(CHIPS, 2, CHUNK)

    pl.semaphore_wait(barrier, CHIPS)

    exchange = [
        remote(seg, segb.at[core], ex_send.at[0], ex_recv.at[0], sibling),
        remote(
            q.at[:, cols(other, HALF)], qb.at[rows_of(core), :], ex_send.at[1], ex_recv.at[1], sibling
        ),
        remote(
            k.at[:, cols(other, KV_HALF)], kb.at[rows_of(core), :], ex_send.at[2], ex_recv.at[2], sibling
        ),
        remote(
            v.at[:, cols(other, KV_HALF)], vb.at[rows_of(core), :], ex_send.at[3], ex_recv.at[3], sibling
        ),
    ]
    for c in exchange:
        c.start()

    def scatter(packets, landing, send, recv):
        here = local(packets.at[chip], landing.at[core, 0], recv.at[0])
        here.start()

        def one(i, there):
            group_of = i // PER_GROUP if isinstance(i, int) else lax.shift_right_logical(i, 3)
            remote(packets.at[there], landing.at[core, i], send, recv.at[group_of], (there, core)).start()

        each_chip(one)

    def scattered(packets, landing, send, recv):
        remote(
            packets.at[pl.ds(0, CHIPS - 1)], landing.at[core, pl.ds(0, CHIPS - 1)], send, recv.at[0], sibling
        ).wait_send()

    def group(i):
        return pl.ds(i * PER_GROUP, PER_GROUP)

    def forward(landing, i, send, recv):
        return remote(
            landing.at[core, group(i)], landing.at[core, group(i)], send.at[i], recv.at[i], sibling
        )

    def hand_on(landing, i, recv, send_f, recv_f):
        block = landing.at[core, group(i)]
        local(block, block, recv.at[i]).wait()
        forward(landing, i, send_f, recv_f).start()

    def arrive(landing, send_f, recv_f):
        def one(i, c):
            theirs = landing.at[other, group(i)]
            remote(theirs, theirs, send_f.at[i], recv_f.at[i], sibling).wait_recv()
            return c

        lax.fori_loop(0, GROUPS, one, 0)

    def hand_on_all(landing, recv, send_f, recv_f):
        def one(i, c):
            hand_on(landing, i, recv, send_f, recv_f)
            return c

        lax.fori_loop(0, GROUPS, one, 0)
        arrive(landing, send_f, recv_f)

    scatter(pkv, kvr, kv_send, kv_recv)

    for unit in range(UNITS):
        a_load((gw, uw)[unit % 2], unit // 2, unit).start()
    for unit in range(4, B_SLOTS):
        b_load((gw, uw)[unit % 2], unit // 2, unit).start()

    for c in ins[3:7]:
        c.wait()
    for c in exchange[:3]:
        c.wait_recv()
    two = 2 * ROWS
    t_at = lax.broadcasted_iota(jnp.int32, (two, two), 0)
    s_at = lax.broadcasted_iota(jnp.int32, (two, two), 1)
    last = jnp.concatenate([segb[0], segb[1]], axis=1) - chip * two
    allowed = (s_at <= t_at) & (last >= t_at)
    for h in range(OWN_HEADS):
        own = pl.ds(h * HEAD, HEAD)
        key = pl.ds(h // 2 * HEAD, HEAD)
        raw = lax.dot_general(
            qb[:, own], kb[:, key], (((1,), (1,)), ((), ())), preferred_element_type=F32
        )
        scores = CAP * jnp.tanh(raw * (HEAD**-0.5 / CAP))
        probs = jnp.where(allowed, jnp.exp(scores), 0.0)
        totals = jnp.sum(probs, axis=-1, keepdims=True)
        if h == 0:
            exchange[3].wait_recv()
        mixed = jnp.dot(probs.astype(BF), vb[:, key], preferred_element_type=F32)
        att[:, own] = (mixed * (1.0 / totals)).astype(BF)

    def halves(landing, j, send, recv):
        return remote(
            part.at[rows_of(other), cols(j)], landing.at[:, cols(j)], send.at[j], recv.at[j], sibling
        )

    def project(j, c):
        o_load(j).wait()
        w = wrows(B_BASE + j * HALF, HALF)[...]
        part[:, cols(j)] = jnp.dot(att[...], w, preferred_element_type=F32).astype(BF)
        halves(prec, j, pr_send, pr_recv).start()
        return c

    lax.fori_loop(0, CHUNKS - 1, project, 0)
    o_load(CHUNKS - 1).wait()

    def end_project(rows):
        w = wrows(B_BASE + (CHUNKS - 1) * HALF, HALF)[...]
        part[rows, cols(CHUNKS - 1)] = jnp.dot(att[rows, :], w, preferred_element_type=F32).astype(BF)

    end_project(rows_of(other))
    halves(prec, CHUNKS - 1, pr_send, pr_recv).start()
    end_project(rows_of(core))
    for unit in range(4):
        b_load((gw, uw)[unit % 2], unit // 2, unit).start()

    def sum_halves(j, squares):
        halves(prec, j, pr_send, pr_recv).wait_recv()
        both = part[rows_of(core), cols(j)].astype(F32) + prec[:, cols(j)].astype(F32)
        gacc[0:ROWS, cols(j)] = both
        return squares + lanes_sum(both * both)

    squares = lax.fori_loop(0, CHUNKS, sum_halves, jnp.zeros((ROWS, 128), F32))
    scale = lax.rsqrt(jnp.sum(squares, axis=-1, keepdims=True) * (1.0 / WIDTH) + EPS)

    def to_packets(packets, first):
        def one(j, c):
            at = cols(first + j)
            added = gacc[0:ROWS, at] * scale * ag_row[at].reshape(1, CHUNK)
            stream = (rb[:, at].astype(F32) + added).astype(BF)
            y_rows = jnp.dot(pick, stream, preferred_element_type=F32).astype(BF)
            packets[:, :, cols(j)] = y_rows.reshape(CHIPS, 2, CHUNK)
            return c

        return one

    for c in ins[7:]:
        c.wait()
    lax.fori_loop(0, FIRST, to_packets(pka, 0), 0)
    scatter(pka, sta, sa_send, sa_recv)
    lax.fori_loop(0, SECOND, to_packets(pkb, FIRST), 0)

    hand_on_all(kvr, kv_recv, kvf_send, kvf_recv)
    at = kvr[:, :, :, KV_WIDTH:].reshape(two, 128).astype(F32)
    at = jnp.transpose(at)[0:1, :].astype(jnp.int32)
    place = (t_at == at).astype(BF)
    own_place = (t_at[0:ROWS, :] + core * ROWS == at).astype(BF)
    for j in range(KV_WIDTH // CHUNK):
        got = jnp.dot(
            own_place, kvr[:, :, :, cols(j)].reshape(two, CHUNK), preferred_element_type=F32
        ).astype(BF)
        kvo[2 * j] = got[:, 0:HEAD]
        kvo[2 * j + 1] = got[:, HEAD:]

    def put(landing, first):
        def one(j, squares):
            rows = landing[:, :, :, cols(j)].reshape(two, CHUNK)
            got = jnp.dot(place, rows, preferred_element_type=F32)
            at = cols(first + j)
            xb[:, at] = (got * pg_row[at].reshape(1, CHUNK)).astype(BF)
            own_rows[:, at] = jnp.dot(own_place, rows, preferred_element_type=F32).astype(BF)
            return squares + lanes_sum(got * got)

        return one

    scatter(pkb, stb, sb_send, sb_recv)
    hand_on_all(sta, sa_recv, saf_send, saf_recv)
    squares = lax.fori_loop(0, FIRST, put(sta, 0), jnp.zeros((two, 128), F32))

    def product(first, depth, start, i):
        w = wbuf[pl.ds(pl.multiple_of(start, CHUNK), depth), pl.ds(i * 256, 256)]
        return jnp.dot(xb[:, pl.ds(first, depth)], w, preferred_element_type=F32)

    def at256(j, i):
        return pl.ds(pl.multiple_of(j * CHUNK + i * 256, 256), 256)

    def begin(j, c):
        for m in range(2):
            a_load(gw, j, 2 * j + m).wait()
        for i in range(CHUNK // 256):
            gacc[:, at256(j, i)] = product(0, A_ROWS, 2 * j * A_ROWS, i)
            uacc[:, at256(j, i)] = product(0, A_ROWS, (2 * j + 1) * A_ROWS, i)

        @pl.when(j > 0)
        def _():
            d_load(j - 1).start()

        hand_on(stb, j, sb_recv, sbf_send, sbf_recv)
        return c

    lax.fori_loop(0, CHUNKS, begin, 0)
    hand_on(stb, CHUNKS, sb_recv, sbf_send, sbf_recv)
    arrive(stb, sbf_send, sbf_recv)
    squares = lax.fori_loop(0, SECOND, put(stb, FIRST), squares)
    scale = lax.rsqrt(jnp.sum(squares, axis=-1, keepdims=True) * (1.0 / WIDTH) + EPS)

    def hidden(j, c):
        for m in range(2):
            b_load(gw, j, 2 * j + m).wait()
        for i in range(CHUNK // 256):
            at = at256(j, i)
            u = (gacc[:, at] + product(A_ROWS, B_ROWS, b_start(2 * j), i)) * scale
            up = (uacc[:, at] + product(A_ROWS, B_ROWS, b_start(2 * j + 1), i)) * scale
            gelu = 0.5 * u * (1.0 + jnp.tanh(0.7978845608028654 * (u + 0.044715 * (u * u * u))))
            act[:, at] = (gelu * up).astype(BF)

        @pl.when(j < CHUNKS - B_SLOTS // 2)
        def _():
            b_load(gw, j + B_SLOTS // 2, 2 * j + B_SLOTS).start()
            b_load(uw, j + B_SLOTS // 2, 2 * j + 1 + B_SLOTS).start()

        @pl.when(j == CHUNKS - B_SLOTS // 2)
        def _():
            d_load(CHUNKS - 1).start()

        return c

    lax.fori_loop(0, CHUNKS, hidden, 0)

    def projected(j, c):
        halves(prec, j, pr_send, pr_recv).wait_send()
        return c

    lax.fori_loop(0, CHUNKS, projected, 0)

    def kept(j):
        return local(part.at[rows_of(core), cols(j)], mine.at[:, cols(j)], keep_sem.at[j])

    def down(j, c):
        d_load(j).wait()
        for i in range(CHUNK // 256):
            w = wbuf[pl.ds(pl.multiple_of(d_start(j), CHUNK), WIDTH), pl.ds(i * 256, 256)]
            part[:, at256(j, i)] = jnp.dot(act[...], w, preferred_element_type=F32).astype(BF)
        halves(theirs, j, dn_send, dn_recv).start()
        kept(j).start()
        return c

    lax.fori_loop(0, CHUNKS - 1, down, 0)
    end = CHUNKS - 1
    d_load(end).wait()

    def end_product(rows, i):
        w = wbuf[pl.ds(B_BASE + 6 * B_ROWS, WIDTH), pl.ds(i * 256, 256)]
        return jnp.dot(act[rows, :], w, preferred_element_type=F32).astype(BF)

    for i in range(CHUNK // 256):
        part[rows_of(other), pl.ds(end * CHUNK + i * 256, 256)] = end_product(rows_of(other), i)
    halves(theirs, end, dn_send, dn_recv).start()
    for i in range(CHUNK // 256):
        mine[:, pl.ds(end * CHUNK + i * 256, 256)] = end_product(rows_of(core), i)

    for c in exchange:
        c.wait_send()
    scattered(pkv, kvr, kv_send, kv_recv)
    scattered(pka, sta, sa_send, sa_recv)
    scattered(pkb, stb, sb_send, sb_recv)

    def sent(i, c):
        forward(kvr, i, kvf_send, kvf_recv).wait_send()
        forward(sta, i, saf_send, saf_recv).wait_send()
        forward(stb, i, sbf_send, sbf_recv).wait_send()
        return c

    lax.fori_loop(0, GROUPS, sent, 0)

    def down_sent(j, c):
        halves(theirs, j, dn_send, dn_recv).wait()
        return c

    lax.fori_loop(0, CHUNKS, down_sent, 0)

    def kept_all(j, c):
        kept(j).wait()
        return c

    lax.fori_loop(0, CHUNKS - 1, kept_all, 0)


def last(mine, theirs, own_rows, kvo, og, lo, kc, vc, rows, og_row, kv_sem, og_sem, out_sem):
    def copy(src, dst, sem):
        return pltpu.make_async_copy(src, dst, sem)

    gain = copy(og, og_row, og_sem)
    gain.start()
    caches = [
        copy(kvo.at[pl.ds(0, 4)], kc, kv_sem.at[0]),
        copy(kvo.at[pl.ds(4, 4)], vc, kv_sem.at[1]),
    ]
    for c in caches:
        c.start()
    squares = jnp.zeros((ROWS, 128), F32)
    for j in range(CHUNKS):
        both = mine[:, cols(j)].astype(F32) + theirs[:, cols(j)].astype(F32)
        squares = squares + lanes_sum(both * both)
    scale = lax.rsqrt(jnp.sum(squares, axis=-1, keepdims=True) * (1.0 / WIDTH) + EPS)
    gain.wait()

    def store(j):
        return copy(rows.at[:, cols(j)], lo.at[:, cols(j)], out_sem.at[j])

    for j in range(CHUNKS):
        both = mine[:, cols(j)].astype(F32) + theirs[:, cols(j)].astype(F32)
        row = og_row[cols(j)].reshape(1, CHUNK)
        rows[:, cols(j)] = (own_rows[:, cols(j)].astype(F32) + both * scale * row).astype(BF)
        store(j).start()
    for j in range(CHUNKS):
        store(j).wait()
    for c in caches:
        c.wait()


def per_device(
    queries,
    keys,
    values,
    residual,
    segment_ids,
    regroup,
    out_weight,
    attn_gain,
    pre_gain,
    gate_weight,
    up_weight,
    down_weight,
    post_gain,
):
    dma = pltpu.SemaphoreType.DMA
    vmem = pltpu.VMEM
    mine, theirs, own_rows, kvo = pl.pallas_call(
        kernel,
        out_shape=(
            vmem((ROWS, WIDTH), BF),
            vmem((ROWS, WIDTH), BF),
            vmem((ROWS, WIDTH), BF),
            vmem((8, ROWS, HEAD), BF),
        ),
        in_specs=[pl.BlockSpec(memory_space=pl.ANY)] * 12,
        out_specs=(pl.BlockSpec(memory_space=vmem),) * 4,
        scratch_shapes=[
            vmem((B_BASE + B_SLOTS * B_ROWS, CHUNK), BF),
            vmem((2 * ROWS, HALF), BF),
            vmem((2 * ROWS, KV_HALF), BF),
            vmem((2 * ROWS, KV_HALF), BF),
            vmem((2, 1, ROWS), jnp.int32),
            vmem((ROWS, KV_WIDTH), BF),
            vmem((1, ROWS), jnp.int32),
            vmem((WIDTH,), F32),
            vmem((WIDTH,), F32),
            vmem((ROWS, WIDTH), BF),
            vmem((2 * ROWS, HALF), BF),
            vmem((2 * ROWS, WIDTH), BF),
            vmem((ROWS, WIDTH), BF),
            vmem((CHIPS, 2, KV_WIDTH + 128), BF),
            vmem((2, CHIPS, 2, KV_WIDTH + 128), BF),
            vmem((CHIPS, 2, A_ROWS), BF),
            vmem((CHIPS, 2, B_ROWS), BF),
            vmem((2, CHIPS, 2, A_ROWS), BF),
            vmem((2, CHIPS, 2, B_ROWS), BF),
            vmem((2 * ROWS, WIDTH), BF),
            vmem((2 * ROWS, WIDTH), BF),
            vmem((2 * ROWS, WIDTH), F32),
            vmem((2 * ROWS, WIDTH), F32),
            dma((10,)),
            dma((CHUNKS,)),
            dma((UNITS,)),
            dma((UNITS,)),
            dma((CHUNKS,)),
            dma((CHUNKS,)),
            dma((4,)),
            dma((4,)),
            dma((CHUNKS,)),
            dma((CHUNKS,)),
            dma((CHUNKS,)),
            dma((CHUNKS,)),
            *[dma, dma((GROUPS,)), dma((GROUPS,)), dma((GROUPS,))] * 3,
        ],
        compiler_params=pltpu.CompilerParams(
            collective_id=0, has_side_effects=True, vmem_limit_bytes=60 * 1024 * 1024
        ),
        name="layer",
    )(
        queries,
        keys,
        values,
        residual,
        segment_ids.reshape(1, ROWS),
        regroup.reshape(1, ROWS),
        out_weight,
        attn_gain,
        pre_gain,
        gate_weight,
        up_weight,
        down_weight,
    )
    return pl.pallas_call(
        last,
        out_shape=(
            jax.ShapeDtypeStruct((ROWS, WIDTH), BF),
            jax.ShapeDtypeStruct((4, ROWS, HEAD), BF),
            jax.ShapeDtypeStruct((4, ROWS, HEAD), BF),
        ),
        in_specs=[pl.BlockSpec(memory_space=vmem)] * 4 + [pl.BlockSpec(memory_space=pl.ANY)],
        out_specs=(pl.BlockSpec(memory_space=pl.ANY),) * 3,
        scratch_shapes=[
            vmem((ROWS, WIDTH), BF),
            vmem((WIDTH,), F32),
            dma((2,)),
            dma,
            dma((CHUNKS,)),
        ],
        compiler_params=pltpu.CompilerParams(vmem_limit_bytes=60 * 1024 * 1024),
        name="last",
    )(*(pltpu.with_memory_space_constraint(r, vmem) for r in (mine, theirs, own_rows, kvo)), post_gain)


def solution(mesh):
    rows = P(("req", "kv"), None)
    flat = P(("req", "kv"))
    return jax.shard_map(
        per_device,
        mesh=mesh,
        in_specs=(
            rows, rows, rows, rows, flat, flat, P("kv", None), P(), P(),
            P(None, "kv"), P(None, "kv"), P("kv", None), P(),
        ),
        out_specs=(rows, P(None, ("req", "kv"), None), P(None, ("req", "kv"), None)),
        check_vma=False,
    )
```
